512 devices in a mesh: fsdp: 32 (over z_lo, x, core), cp: 16 (over y, z_hi).
Axes of the slice: x: 4, y: 8, z: 8 (z_hi: 2, z_lo: 4; z = z_hi * 4 + z_lo), core: 2. Of those that a mesh axis runs over, the one named last changes fastest.
Arguments:
- queries: bfloat16 [4096, 16384], P('cp', 'fsdp'), may hold values from -8 to 8
- key_vectors: bfloat16 [4096, 1024], P(('fsdp', 'cp')), may hold values from -8 to 8
- value_vectors: bfloat16 [4096, 1024], P(('fsdp', 'cp')), may hold values from -6 to 6
- out_grads: bfloat16 [4096, 16384], P('cp', 'fsdp'), may hold values from -6 to 6
- pair_order: int32 [32], replicated, may hold values from 0 to 31, as said below
Outputs:
- attended: bfloat16 [4096, 16384], P('cp', 'fsdp')
- query_grads: bfloat16 [4096, 16384], P('cp', 'fsdp')
- key_grads: float32 [4096, 1024], P(('fsdp', 'cp'))
- value_grads: float32 [4096, 1024], P(('fsdp', 'cp'))
The draws below stay inside these ranges and needn't reach their ends.
Inputs may be any that keep to these rules, and one draw needn't show every extreme that they name: `pair_order`: A permutation of the stretches; slots 2 c and 2 c + 1 hold stretches P and 31 - P for some P, in either order.
All inputs are finite; a program needn't handle non-finite values.
Results may differ from the reference program's by a relative error of at most 0.034.
Values may be sent and summed in bfloat16 or wider, within the bound.
No kernel may reach another device: no remote copies, remote signals or barrier semaphores. Data moves between devices by JAX's collectives and lax.ppermute only.
A program may use at most 64 MiB of HBM per device.

```python
import math
import jax
import jax.numpy as jnp
from jax import lax

HD = 128
TOK_DEV = 256
HEADS = 128
KV_HEADS = 8
SEQ = 4096
N_CP = 16


def draw_queries(key, part):
    base = jnp.clip(jax.random.normal(jax.random.fold_in(key, 1), (SEQ, HEADS * HD), jnp.float32), -6.0, 6.0)
    return base.astype(jnp.bfloat16)


def draw_key_vectors(key, part):
    base = jnp.clip(jax.random.normal(jax.random.fold_in(key, 2), (SEQ, KV_HEADS * HD), jnp.float32), -6.0, 6.0)
    return base.astype(jnp.bfloat16)


def draw_pair_order(key, part):
    early = jax.random.permutation(jax.random.fold_in(key, 41), N_CP).astype(jnp.int32)
    late = (2 * N_CP - 1 - early).astype(jnp.int32)
    flips = jax.random.randint(jax.random.fold_in(key, 42), (N_CP,), 0, 2, jnp.int32)
    first = jnp.where(flips == 1, late, early)
    second = jnp.where(flips == 1, early, late)
    return jnp.stack([first, second], axis=1).reshape(2 * N_CP).astype(jnp.int32)


def steps_of(key, dims, cuts, least, high):
    def one(position, blocks):
        draws = jax.random.uniform(jax.random.fold_in(jax.random.fold_in(key, 6), position), (blocks,), jnp.float32, least / len(cuts), high / len(cuts))
        return jnp.repeat(jnp.exp(draws), dims[position] // blocks).reshape((-1,) + (1,) * (len(dims) - position - 1))

    gain = one(*cuts[0])
    for cut in cuts[1:]:
        gain = gain * one(*cut)
    return gain


def centred(rng, shape, scale, reach, shards=(), held_as=jnp.bfloat16):
    factor_of = steps_of(rng, shape, shards, -0.22, 0.18) if shards else 1.0
    entries = jax.random.normal(rng, shape, jnp.float32) * scale * factor_of
    return jnp.minimum(jnp.maximum(entries, -reach), reach).astype(held_as)


def setup_inputs(seed: int = 0) -> dict:
    arg_keys = jax.random.split(jax.random.key(seed), 6)
    queries = draw_queries(jax.random.fold_in(arg_keys[5], 71), 0)
    key_vectors = draw_key_vectors(jax.random.fold_in(arg_keys[5], 71), 0)
    value_vectors = centred(arg_keys[2], (SEQ, KV_HEADS * HD), 1.0, 6.0, ((0, 512),))
    out_grads = centred(arg_keys[3], (SEQ, HEADS * HD), 1.0, 6.0, ((0, 16), (1, 32)))
    pair_order = draw_pair_order(jax.random.fold_in(arg_keys[5], 71), 0)
    return {"queries": queries, "key_vectors": key_vectors, "value_vectors": value_vectors, "out_grads": out_grads, "pair_order": pair_order}


NEG_FILL = -1e+30

def layout_positions(pair_order):
    rows = jnp.arange(SEQ, dtype=jnp.int32)
    half_rows = TOK_DEV // 2
    slot = rows // half_rows
    stretch = pair_order[slot].astype(jnp.int32)
    return (stretch * half_rows + rows % half_rows).astype(jnp.int32)

def reference(queries, key_vectors, value_vectors, out_grads, pair_order):
    positions = layout_positions(pair_order)
    visible = jnp.arange(SEQ, dtype=jnp.int32)[None, :] <= positions[:, None]
    group_size = HEADS // KV_HEADS
    score_scale = 1.0 / math.sqrt(HD)
    query_heads = queries.reshape(SEQ, HEADS, HD).transpose(1, 0, 2)
    grad_heads = out_grads.reshape(SEQ, HEADS, HD).transpose(1, 0, 2)
    key_heads = key_vectors.reshape(SEQ, KV_HEADS, HD).transpose(1, 0, 2)
    value_heads = value_vectors.reshape(SEQ, KV_HEADS, HD).transpose(1, 0, 2)

    def per_head(head_index):
        kv_index = head_index // group_size
        query_one = query_heads[head_index]
        grad_one = grad_heads[head_index]
        key_one = key_heads[kv_index]
        value_one = value_heads[kv_index]
        scores = jnp.dot(query_one, key_one.T, preferred_element_type=jnp.float32) * score_scale
        masked = jnp.where(visible, scores, NEG_FILL)
        row_peak = lax.optimization_barrier(jnp.max(masked, axis=1, keepdims=True))
        log_total = row_peak + jnp.log(lax.optimization_barrier(jnp.sum(jnp.exp(masked - row_peak), axis=1, keepdims=True)))
        prob_exact = jnp.where(visible, jnp.exp(scores - log_total), 0.0)
        prob_half = prob_exact.astype(jnp.bfloat16)
        output = jnp.dot(prob_half, value_one, preferred_element_type=jnp.float32).astype(jnp.bfloat16)
        row_delta = lax.optimization_barrier(jnp.sum(grad_one.astype(jnp.float32) * output.astype(jnp.float32), axis=1, keepdims=True))
        prob_grad = jnp.dot(grad_one, value_one.T, preferred_element_type=jnp.float32)
        score_grad = (prob_exact * (prob_grad - row_delta) * score_scale).astype(jnp.bfloat16)
        query_grad = jnp.dot(score_grad, key_one, preferred_element_type=jnp.float32).astype(jnp.bfloat16)
        key_grad = jnp.dot(score_grad.T, query_one, preferred_element_type=jnp.float32)
        value_grad = jnp.dot(prob_half.T, grad_one, preferred_element_type=jnp.float32)
        return (output, query_grad, key_grad, value_grad)
    outputs, query_grad, key_grad, value_grad = lax.map(per_head, jnp.arange(HEADS, dtype=jnp.int32))
    attended = outputs.transpose(1, 0, 2).reshape(SEQ, HEADS * HD)
    query_grads = query_grad.transpose(1, 0, 2).reshape(SEQ, HEADS * HD)
    key_sum = key_grad.reshape(KV_HEADS, group_size, SEQ, HD).sum(axis=1)
    value_sum = value_grad.reshape(KV_HEADS, group_size, SEQ, HD).sum(axis=1)
    key_grads = key_sum.transpose(1, 0, 2).reshape(SEQ, KV_HEADS * HD)
    value_grads = value_sum.transpose(1, 0, 2).reshape(SEQ, KV_HEADS * HD)
    return (attended, query_grads, key_grads, value_grads)
```

```python
import math
import jax
import jax.numpy as jnp
from jax import lax
from jax.experimental import pallas as pl
from jax.experimental.pallas import tpu as pltpu
from jax.sharding import Mesh, PartitionSpec as P

HD = 128
BF16 = jnp.bfloat16
F32 = jnp.float32


def nn(a, b):
    return jnp.dot(a, b, preferred_element_type=F32)


def tn(a, b):
    return lax.dot_general(a, b, (((0,), (0,)), ((), ())), preferred_element_type=F32)


def flip(x):
    return x.astype(F32).T


def attention_kernel(
    order_ref,
    q_ref,
    g_ref,
    mine_ref,
    theirs_ref,
    out_ref,
    dq_ref,
    dmine_ref,
    dtheirs_ref,
    s_ref,
    e_ref,
    qn_ref,
    qt_ref,
    gn_ref,
    gt_ref,
    acc_ref,
    delta_ref,
):
    half = q_ref.shape[0] // 2
    heads = q_ref.shape[1] // HD
    cols = heads * half
    runs, pairs, _, grain, _ = mine_ref.shape
    scale = 1.0 / math.sqrt(HD)
    rate = scale * math.log2(math.e)
    core = lax.axis_index("core")
    first = 2 * (lax.axis_index("y") * lax.axis_size("zh") + lax.axis_index("zh"))
    late = jnp.where(order_ref[first + 1] > order_ref[first], 1, 0)
    stretches = (order_ref[first + late], order_ref[first + 1 - late])
    offsets = (
        pl.multiple_of(late * half, half),
        pl.multiple_of((1 - late) * half, half),
    )
    counts = tuple(lax.shift_right_logical(s, 1) + 1 for s in stretches)

    def rows_of(index, which):
        parts = (mine_ref[:, index, which], theirs_ref[:, index, which])
        return jnp.concatenate([p.reshape(half, HD) for p in parts], axis=0)

    for t in range(2):
        for h in range(heads):
            span = slice(t * cols + h * half, t * cols + (h + 1) * half)
            block = q_ref[pl.ds(offsets[t], half), h * HD : (h + 1) * HD]
            qn_ref[span, :] = block
            qt_ref[:, span] = flip(block).astype(BF16)

    for t in range(2):
        span = slice(t * cols, (t + 1) * cols)
        base = 0 if t == 0 else pairs

        def score(index, peak, masked):
            s = nn(rows_of(index, 0), qt_ref[:, span])
            if masked:
                j = lax.broadcasted_iota(jnp.int32, s.shape, 0)
                r = lax.broadcasted_iota(jnp.int32, s.shape, 1)
                shift = jnp.where(j < half, core * half, -core * half)
                row = lax.rem(r, half) + lax.rem(stretches[t], 2) * half
                s = jnp.where(j + shift <= row, s, -1e30)
            s_ref[index] = s
            return jnp.maximum(peak, jnp.max(s.reshape(-1, 8, cols), axis=0))

        last = counts[t] - 1
        peak = jnp.full((8, cols), -1e30, F32)
        peak = lax.fori_loop(0, last, lambda i, p: score(i, p, False), peak)
        peak = score(last, peak, True)
        shift = jnp.max(peak, axis=0, keepdims=True) * rate

        acc_ref[t] = jnp.zeros((HD, cols), F32)

        def weigh(index, total):
            e = jnp.exp2(s_ref[index] * rate - shift)
            total = total + jnp.sum(e.reshape(-1, 8, cols), axis=0)
            weight = e.astype(BF16)
            e_ref[base + index] = weight
            acc_ref[t] += tn(rows_of(index, 1), weight)
            return total

        total = lax.fori_loop(0, counts[t], weigh, jnp.zeros((8, cols), F32))
        inverse = 1.0 / jnp.sum(total, axis=0, keepdims=True)
        for h in range(heads):
            part = slice(h * half, (h + 1) * half)
            full = slice(t * cols + h * half, t * cols + (h + 1) * half)
            column = slice(h * HD, (h + 1) * HD)
            out = (acc_ref[t, :, part] * inverse[:, part]).astype(BF16)
            out_ref[pl.ds(offsets[t], half), column] = flip(out).astype(BF16)
            grad = flip(g_ref[pl.ds(offsets[t], half), column]) * inverse[:, part]
            half_grad = grad.astype(BF16)
            gt_ref[:, full] = half_grad
            gn_ref[full, :] = flip(half_grad).astype(BF16)
            delta = jnp.sum(grad * out.astype(F32), axis=0, keepdims=True)
            delta_ref[t, :, part] = delta
        acc_ref[t] = jnp.zeros((HD, cols), F32)

    def store(index, which, value):
        value = value.astype(BF16)
        shape = (runs, grain, HD)
        dmine_ref[:, index, which] = value[:half].reshape(shape)
        dtheirs_ref[:, index, which] = value[half:].reshape(shape)

    def pull(index, both):
        keys = rows_of(index, 0)
        values = rows_of(index, 1)
        key_term = jnp.zeros((2 * half, HD), F32)
        value_term = jnp.zeros((2 * half, HD), F32)
        for t in range(2 if both else 1):
            span = slice(t * cols, (t + 1) * cols)
            weight = e_ref[index if t == 0 else pairs + index]
            slope = nn(values, gt_ref[:, span]) - delta_ref[t]
            ds = (weight.astype(F32) * slope).astype(BF16)
            value_term = value_term + nn(weight, gn_ref[span, :])
            key_term = key_term + nn(ds, qn_ref[span, :])
            acc_ref[t] += tn(keys, ds)
        store(index, 0, key_term * scale)
        store(index, 1, value_term)

    @pl.loop(0, counts[1])
    def _(index):
        pull(index, True)

    @pl.loop(counts[1], counts[0])
    def _(index):
        pull(index, False)

    @pl.loop(counts[0], pairs)
    def _(index):
        for which in range(2):
            store(index, which, jnp.zeros((2 * half, HD), F32))

    for t in range(2):
        for h in range(heads):
            part = slice(h * half, (h + 1) * half)
            value = (acc_ref[t, :, part] * scale).T.astype(BF16)
            dq_ref[pl.ds(offsets[t], half), h * HD : (h + 1) * HD] = value


def attention(order, queries, grads, mine, theirs):
    rows, width = queries.shape
    half, cols, pairs = rows // 2, width // HD * (rows // 2), mine.shape[1]
    vmem = pl.BlockSpec(memory_space=pltpu.VMEM)
    return pl.pallas_call(
        attention_kernel,
        out_shape=(
            jax.ShapeDtypeStruct(queries.shape, BF16),
            jax.ShapeDtypeStruct(queries.shape, BF16),
            jax.ShapeDtypeStruct(mine.shape, BF16),
            jax.ShapeDtypeStruct(mine.shape, BF16),
        ),
        in_specs=[pl.BlockSpec(memory_space=pltpu.SMEM)] + [vmem] * 4,
        out_specs=(vmem,) * 4,
        scratch_shapes=[
            pltpu.VMEM((pairs, 2 * half, cols), F32),
            pltpu.VMEM((pairs + pairs // 2, 2 * half, cols), BF16),
            pltpu.VMEM((2 * cols, HD), BF16),
            pltpu.VMEM((HD, 2 * cols), BF16),
            pltpu.VMEM((2 * cols, HD), BF16),
            pltpu.VMEM((HD, 2 * cols), BF16),
            pltpu.VMEM((2, HD, cols), F32),
            pltpu.VMEM((2, 1, cols), F32),
        ],
        compiler_params=pltpu.CompilerParams(vmem_limit_bytes=48 << 20),
        name="attention",
    )(order, queries, grads, mine, theirs)


AXES = ("zl", "xh", "xl", "core", "y", "zh")
SPREAD = ("zl", "xh", "xl", "zh")
SWAP = ((0, 1), (1, 0))


def per_device(queries, key_vectors, value_vectors, out_grads, pair_order):
    sizes = {name: lax.axis_size(name) for name in AXES}
    zl, xh, xl, zh = (sizes[name] for name in SPREAD)
    rows = key_vectors.shape[0]
    kv_heads = key_vectors.shape[1] // HD
    runs = sizes["y"]
    pairs = zl * xh * xl

    both = jnp.stack([key_vectors, value_vectors]).reshape(2, rows, kv_heads, HD)
    sent = both.transpose(2, 0, 1, 3).reshape(zl, xh, 1, 1, 2, rows, HD)
    sent = jnp.broadcast_to(sent, (zl, xh, xl, zh, 2, rows, HD))
    sent = sent.reshape(pairs * zh, 2, rows, HD)
    got = lax.all_to_all(sent, SPREAD, split_axis=0, concat_axis=0, tiled=True)
    run = got.reshape(pairs, zh, 2, rows, HD).transpose(0, 2, 1, 3, 4)
    run = run.reshape(1, pairs, 2, zh * rows, HD)
    whole = jnp.broadcast_to(run, (runs,) + run.shape[1:])
    mine = lax.all_to_all(whole, "y", split_axis=0, concat_axis=0, tiled=True)
    theirs = lax.ppermute(mine, "core", SWAP)

    attended, query_grads, dmine, dtheirs = attention(
        pair_order, queries, out_grads, mine, theirs
    )

    other = lax.ppermute(dtheirs, "core", SWAP)
    total = (dmine.astype(F32) + other.astype(F32)).astype(BF16)
    got = lax.all_to_all(total, "y", split_axis=0, concat_axis=0, tiled=True)
    total = got.astype(F32).sum(axis=0).astype(BF16)
    total = total.reshape(pairs, 2, zh, rows, HD).transpose(0, 2, 1, 3, 4)
    total = total.reshape(pairs * zh, 2, rows, HD)
    got = lax.all_to_all(total, SPREAD, split_axis=0, concat_axis=0, tiled=True)
    total = got.reshape(kv_heads, xl * zh, 2, rows, HD).astype(F32).sum(axis=1)
    total = total.transpose(1, 2, 0, 3).reshape(2, rows, kv_heads * HD)
    return attended, query_grads, total[0], total[1]


def solution(mesh):
    fine = Mesh(mesh.devices.reshape(4, 2, 2, 2, 8, 2), AXES)
    fsdp, cp = AXES[:4], AXES[4:]
    return jax.shard_map(
        per_device,
        mesh=fine,
        in_specs=(P(cp, fsdp), P(AXES, None), P(AXES, None), P(cp, fsdp), P()),
        out_specs=(P(cp, fsdp), P(cp, fsdp), P(AXES, None), P(AXES, None)),
        check_vma=False,
    )
```

```python
import math
import jax
import jax.numpy as jnp
from jax import lax
from jax.experimental import pallas as pl
from jax.experimental.pallas import tpu as pltpu
from jax.sharding import Mesh, PartitionSpec as P

HD = 128
BF16 = jnp.bfloat16
F32 = jnp.float32
SCALE = 1.0 / math.sqrt(HD)
RATE = SCALE * math.log2(math.e)
FILL = -1e30
VMEM_BYTES = 32 << 20


def dot(a, b, a_axis, b_axis):
    return lax.dot_general(
        a, b, (((a_axis,), (b_axis,)), ((), ())), preferred_element_type=F32
    )


def flip(x):
    return x.astype(F32).T


def stretches_of(order_ref, half):
    first = 2 * (lax.axis_index("y") * lax.axis_size("zh") + lax.axis_index("zh"))
    late = jnp.where(order_ref[first + 1] > order_ref[first], 1, 0)
    stretches = (order_ref[first + late], order_ref[first + 1 - late])
    offsets = (
        pl.multiple_of(late * half, half),
        pl.multiple_of((1 - late) * half, half),
    )
    return stretches, offsets


def counts_of(stretches, parity):
    seen = [lax.shift_right_logical(s - parity + 2, 1) for s in stretches]
    return tuple(jnp.maximum(lax.shift_right_logical(n + 1, 1), 1) for n in seen)


def block_of(ref, index, which):
    runs, _, _, grain, _ = ref.shape
    parts = [ref[:, 2 * index + u, which].reshape(runs * grain, HD) for u in range(2)]
    return jnp.concatenate(parts, axis=0)


def forward(keys_ref, parity, stretches, qt_ref, s_ref, e_ref, acc_ref):
    cols = s_ref.shape[2]
    blocks = keys_ref.shape[1] // 2
    half = s_ref.shape[1] // 2
    counts = counts_of(stretches, parity)
    bases = (0, blocks)
    shifts = []
    for t in range(2):
        span = slice(t * cols, (t + 1) * cols)

        def score(index, peak, masked):
            s = dot(block_of(keys_ref, index, 0), qt_ref[:, span], 1, 0)
            if masked:
                j = lax.broadcasted_iota(jnp.int32, s.shape, 0)
                r = lax.rem(lax.broadcasted_iota(jnp.int32, s.shape, 1), half)
                j = j + jnp.where(j >= half, half, 0)
                ahead = (4 * index + parity - stretches[t]) * half
                s = jnp.where(j + ahead <= r, s, FILL)
            s_ref[bases[t] + index] = s
            return jnp.maximum(peak, jnp.max(s.reshape(-1, 8, cols), axis=0))

        last = counts[t] - 1
        peak = jnp.full((8, cols), FILL, F32)
        peak = lax.fori_loop(0, last, lambda i, p: score(i, p, False), peak)
        peak = score(last, peak, True)
        shifts.append(jnp.max(peak, axis=0, keepdims=True) * RATE)

    results = []
    for t in range(2):

        def weigh(index, total):
            e = jnp.exp2(s_ref[bases[t] + index] * RATE - shifts[t])
            e_ref[bases[t] + index] = e.astype(BF16)
            return total + jnp.sum(e.reshape(-1, 8, cols), axis=0)

        def attend(index):
            return dot(block_of(keys_ref, index, 1), e_ref[bases[t] + index], 0, 0)

        def step(index, total):
            acc_ref[t] += attend(index - 1)
            return weigh(index, total)

        acc_ref[t] = jnp.zeros(acc_ref.shape[1:], F32)
        total = weigh(0, jnp.zeros((8, cols), F32))
        total = lax.fori_loop(1, counts[t], step, total)
        acc_ref[t] += attend(counts[t] - 1)
        results.append((shifts[t], jnp.sum(total, axis=0, keepdims=True)))
    return results


def backward(keys_ref, parity, stretches, qt_ref, gt_ref, delta_ref, e_ref, acc_ref, out_ref):
    runs, pairs, _, grain, _ = keys_ref.shape
    cols = qt_ref.shape[1] // 2
    half = runs * grain
    blocks = pairs // 2
    counts = counts_of(stretches, parity)

    def store(index, which, value):
        for u in range(2):
            part = value[u * half : (u + 1) * half].reshape(runs, grain, HD)
            out_ref[:, 2 * index + u, which] = part

    def pull(index, both):
        keys = block_of(keys_ref, index, 0)
        values = block_of(keys_ref, index, 1)
        key_term = value_term = None
        for t in range(2 if both else 1):
            span = slice(t * cols, (t + 1) * cols)
            weight = e_ref[index if t == 0 else blocks + index]
            slope = dot(values, gt_ref[:, span], 1, 0) - delta_ref[t]
            ds = (weight.astype(F32) * slope).astype(BF16)
            acc_ref[t] += dot(keys, ds, 0, 0)
            value_part = dot(gt_ref[:, span], weight, 1, 1)
            key_part = dot(qt_ref[:, span], ds, 1, 1)
            value_term = value_part if t == 0 else value_term + value_part
            key_term = key_part if t == 0 else key_term + key_part
        store(index, 0, (key_term * SCALE).T.astype(BF16))
        store(index, 1, value_term.T.astype(BF16))

    @pl.loop(0, counts[1])
    def _(index):
        pull(index, True)

    @pl.loop(counts[1], counts[0])
    def _(index):
        pull(index, False)

    @pl.loop(counts[0], blocks)
    def _(index):
        for which in range(2):
            store(index, which, jnp.zeros((2 * half, HD), BF16))


def first_kernel(order_ref, q_ref, keys_ref, qt_ref, e_ref, acc_ref, stat_ref, s_ref):
    half = q_ref.shape[0] // 2
    heads = q_ref.shape[1] // HD
    cols = heads * half
    stretches, offsets = stretches_of(order_ref, half)
    for t in range(2):
        for h in range(heads):
            block = q_ref[pl.ds(offsets[t], half), h * HD : (h + 1) * HD]
            start = t * cols + h * half
            qt_ref[:, start : start + half] = flip(block).astype(BF16)
    parity = lax.axis_index("core")
    results = forward(keys_ref, parity, stretches, qt_ref, s_ref, e_ref, acc_ref)
    for t in range(2):
        for k in range(2):
            stat_ref[2 * t + k] = results[t][k]


def second_kernel(
    order_ref,
    g_ref,
    keys_ref,
    qt_ref,
    old_acc_ref,
    old_stat_ref,
    out_ref,
    gt_ref,
    delta_ref,
    dkeys_ref,
    dq_acc_ref,
    s_ref,
    e_ref,
    acc_ref,
    own_gt_ref,
    own_delta_ref,
):
    half = g_ref.shape[0] // 2
    heads = g_ref.shape[1] // HD
    cols = heads * half
    stretches, offsets = stretches_of(order_ref, half)
    parity = 1 - lax.axis_index("core")
    results = forward(keys_ref, parity, stretches, qt_ref, s_ref, e_ref, acc_ref)
    for t in range(2):
        old_shift, old_total = old_stat_ref[2 * t], old_stat_ref[2 * t + 1]
        new_shift, new_total = results[t]
        shift = jnp.maximum(old_shift, new_shift)
        old_part = jnp.exp2(old_shift - shift)
        new_part = jnp.exp2(new_shift - shift)
        inverse = 1.0 / (old_total * old_part + new_total * new_part)
        old_part = old_part * inverse
        new_part = new_part * inverse
        for h in range(heads):
            part = slice(h * half, (h + 1) * half)
            full = slice(t * cols + h * half, t * cols + (h + 1) * half)
            column = slice(h * HD, (h + 1) * HD)
            total = old_acc_ref[t, :, part] * old_part[:, part]
            total = total + acc_ref[t, :, part] * new_part[:, part]
            out = total.astype(BF16)
            out_ref[pl.ds(offsets[t], half), column] = flip(out).astype(BF16)
            grad = flip(g_ref[pl.ds(offsets[t], half), column])
            gt_ref[:, full] = (grad * old_part[:, part]).astype(BF16)
            own_gt_ref[:, full] = (grad * new_part[:, part]).astype(BF16)
            delta = jnp.sum(grad * out.astype(F32), axis=0, keepdims=True)
            delta_ref[t, :, part] = delta * old_part[:, part]
            own_delta_ref[t, :, part] = delta * new_part[:, part]
        dq_acc_ref[t] = jnp.zeros(dq_acc_ref.shape[1:], F32)
    backward(
        keys_ref,
        parity,
        stretches,
        qt_ref,
        own_gt_ref,
        own_delta_ref,
        e_ref,
        dq_acc_ref,
        dkeys_ref,
    )


def third_kernel(
    order_ref,
    keys_ref,
    qt_ref,
    gt_ref,
    delta_ref,
    e_ref,
    old_acc_ref,
    dkeys_ref,
    dq_ref,
    acc_ref,
):
    half = dq_ref.shape[0] // 2
    heads = dq_ref.shape[1] // HD
    stretches, offsets = stretches_of(order_ref, half)
    parity = lax.axis_index("core")
    acc_ref[...] = old_acc_ref[...]
    backward(
        keys_ref,
        parity,
        stretches,
        qt_ref,
        gt_ref,
        delta_ref,
        e_ref,
        acc_ref,
        dkeys_ref,
    )
    for t in range(2):
        for h in range(heads):
            value = (acc_ref[t, :, h * half : (h + 1) * half] * SCALE).T.astype(BF16)
            dq_ref[pl.ds(offsets[t], half), h * HD : (h + 1) * HD] = value


def call(kernel, name, outs, scratch, flops, *args):
    vmem = pl.BlockSpec(memory_space=pltpu.VMEM)
    return pl.pallas_call(
        kernel,
        out_shape=tuple(jax.ShapeDtypeStruct(*out) for out in outs),
        in_specs=[pl.BlockSpec(memory_space=pltpu.SMEM)] + [vmem] * (len(args) - 1),
        out_specs=(vmem,) * len(outs),
        scratch_shapes=[pltpu.VMEM(*item) for item in scratch],
        compiler_params=pltpu.CompilerParams(vmem_limit_bytes=VMEM_BYTES),
        cost_estimate=pl.CostEstimate(
            flops=flops, bytes_accessed=8 << 20, transcendentals=0
        ),
        name=name,
    )(*args)


def shapes_of(queries, keys):
    rows, width = queries.shape
    half = rows // 2
    cols = width // HD * half
    slots = keys.shape[1] // 2 + keys.shape[1] // 4
    weights = (slots, 2 * half, cols)
    return dict(
        weights=(weights, BF16),
        scores=(weights, F32),
        flat=((HD, 2 * cols), BF16),
        acc=((2, HD, cols), F32),
        row=((2, 1, cols), F32),
        stat=((4, 1, cols), F32),
        keys=(keys.shape, BF16),
        queries=(queries.shape, BF16),
    )


def attend_mine(order, queries, mine):
    s = shapes_of(queries, mine)
    outs = (s["flat"], s["weights"], s["acc"], s["stat"])
    return call(
        first_kernel, "first", outs, (s["scores"],), 3 << 30, order, queries, mine
    )


def attend_theirs(order, grads, theirs, qt, acc, stat):
    s = shapes_of(grads, theirs)
    outs = (s["queries"], s["flat"], s["row"], s["keys"], s["acc"])
    scratch = (s["scores"], s["weights"], s["acc"], s["flat"], s["row"])
    return call(
        second_kernel, "second", outs, scratch, 6 << 30, order, grads, theirs, qt, acc, stat
    )


def finish_mine(order, queries, mine, qt, gt, delta, weights, acc):
    s = shapes_of(queries, mine)
    outs = (s["keys"], s["queries"])
    return call(
        third_kernel,
        "third",
        outs,
        (s["acc"],),
        4 << 30,
        order,
        mine,
        qt,
        gt,
        delta,
        weights,
        acc,
    )


AXES = ("zl", "xh", "xl", "core", "y", "zh")
SPREAD = ("zl", "xh", "xl", "zh")
SWAP = ((0, 1), (1, 0))


def per_device(queries, key_vectors, value_vectors, out_grads, pair_order):
    sizes = {name: lax.axis_size(name) for name in AXES}
    zl, xh, xl, zh = (sizes[name] for name in SPREAD)
    rows = key_vectors.shape[0]
    kv_heads = key_vectors.shape[1] // HD
    runs = sizes["y"]
    pairs = zl * xh * xl

    both = jnp.stack([key_vectors, value_vectors]).reshape(2, rows, kv_heads, HD)
    sent = both.transpose(2, 0, 1, 3).reshape(zl, xh, 1, 1, 2, rows, HD)
    sent = jnp.broadcast_to(sent, (zl, xh, xl, zh, 2, rows, HD))
    sent = sent.reshape(pairs * zh, 2, rows, HD)
    got = lax.all_to_all(sent, SPREAD, split_axis=0, concat_axis=0, tiled=True)
    run = got.reshape(pairs, zh, 2, rows, HD).transpose(0, 2, 1, 3, 4)
    run = run.reshape(1, pairs, 2, zh * rows, HD)
    whole = jnp.broadcast_to(run, (runs,) + run.shape[1:])
    mine = lax.all_to_all(whole, "y", split_axis=0, concat_axis=0, tiled=True)
    theirs = lax.ppermute(mine, "core", SWAP)

    qt, weights, acc, stat = attend_mine(pair_order, queries, mine)
    attended, gt, delta, dtheirs, acc = attend_theirs(
        pair_order, out_grads, theirs, qt, acc, stat
    )
    other = lax.ppermute(dtheirs, "core", SWAP)
    dmine, query_grads = finish_mine(
        pair_order, queries, mine, qt, gt, delta, weights, acc
    )
    total = (dmine.astype(F32) + other.astype(F32)).astype(BF16)
    got = lax.all_to_all(total, "y", split_axis=0, concat_axis=0, tiled=True)
    total = got.astype(F32).sum(axis=0).astype(BF16)
    total = total.reshape(pairs, 2, zh, rows, HD).transpose(0, 2, 1, 3, 4)
    total = total.reshape(pairs * zh, 2, rows, HD)
    got = lax.all_to_all(total, SPREAD, split_axis=0, concat_axis=0, tiled=True)
    total = got.reshape(kv_heads, xl * zh, 2, rows, HD).astype(F32).sum(axis=1)
    total = total.transpose(1, 2, 0, 3).reshape(2, rows, kv_heads * HD)
    return attended, query_grads, total[0], total[1]


def solution(mesh):
    fine = Mesh(mesh.devices.reshape(4, 2, 2, 2, 8, 2), AXES)
    fsdp, cp = AXES[:4], AXES[4:]
    return jax.shard_map(
        per_device,
        mesh=fine,
        in_specs=(P(cp, fsdp), P(AXES, None), P(AXES, None), P(cp, fsdp), P()),
        out_specs=(P(cp, fsdp), P(cp, fsdp), P(AXES, None), P(AXES, None)),
        check_vma=False,
    )
```

```python
import math
import jax
import jax.numpy as jnp
from jax import lax
from jax.experimental import pallas as pl
from jax.experimental.pallas import tpu as pltpu
from jax.sharding import Mesh, PartitionSpec as P

HD = 128
BF16 = jnp.bfloat16
F32 = jnp.float32
SCALE = 1.0 / math.sqrt(HD)
RATE = SCALE * math.log2(math.e)
FILL = -1e30
VMEM_BYTES = 32 << 20
CHUNK = 64
GROUP = 4


def dot(a, b, a_axis, b_axis):
    return lax.dot_general(
        a, b, (((a_axis,), (b_axis,)), ((), ())), preferred_element_type=F32
    )


def flip(x):
    return x.astype(F32).T


def stretches_of(order_ref, half):
    first = 2 * (lax.axis_index("y") * lax.axis_size("zh") + lax.axis_index("zh"))
    late = jnp.where(order_ref[first + 1] > order_ref[first], 1, 0)
    stretches = (order_ref[first + late], order_ref[first + 1 - late])
    offsets = (
        pl.multiple_of(late * half, half),
        pl.multiple_of((1 - late) * half, half),
    )
    return stretches, offsets


def counts_of(stretches, parity):
    seen = [lax.shift_right_logical(s - parity + 2, 1) for s in stretches]
    return tuple(jnp.maximum(lax.shift_right_logical(n + 1, 1), 1) for n in seen)


def block_of(ref, index, which):
    runs, _, slices, _, grain, _ = ref.shape
    parts = [
        ref[:, 2 * index + u, :, which].astype(F32).reshape(runs * slices * grain, HD)
        for u in range(2)
    ]
    return jnp.concatenate(parts, axis=0).astype(BF16)


def wide(ref, first, count):
    return jnp.concatenate([ref[first + k] for k in range(count)], axis=1)


def forward(keys_ref, parity, stretches, qt_ref, s_ref, e_ref, acc_ref):
    rows, cols = s_ref.shape[1:]
    blocks = keys_ref.shape[1] // 2
    half = rows // 2
    heads = cols // half
    counts = counts_of(stretches, parity)
    bases = (0, blocks)
    shifts = []
    for t in range(2):

        def score(index, peak, masked):
            keys = block_of(keys_ref, index, 0)
            peaks = []
            for c in range(0, heads, GROUP):
                span = slice(c * half, (c + GROUP) * half)
                s = dot(keys, wide(qt_ref, t * heads + c, GROUP), 1, 0)
                if masked:
                    j = lax.broadcasted_iota(jnp.int32, s.shape, 0)
                    r = lax.rem(lax.broadcasted_iota(jnp.int32, s.shape, 1), half)
                    j = j + jnp.where(j >= half, half, 0)
                    ahead = (4 * index + parity - stretches[t]) * half
                    s = jnp.where(j + ahead <= r, s, FILL)
                s_ref[bases[t] + index, :, span] = s
                high = jnp.max(s.reshape(-1, 8, GROUP * half), axis=0)
                peaks.append(jnp.maximum(peak[:, span], high))
            return jnp.concatenate(peaks, axis=1)

        last = counts[t] - 1
        peak = jnp.full((8, cols), FILL, F32)
        peak = lax.fori_loop(0, last, lambda i, p: score(i, p, False), peak)
        peak = score(last, peak, True)
        shifts.append(jnp.max(peak, axis=0, keepdims=True) * RATE)

    results = []
    for t in range(2):

        def weigh(index, total):
            slot = bases[t] + index
            totals = []
            for h in range(heads):
                span = slice(h * half, (h + 1) * half)
                shift = shifts[t][:, span]
                part = total[:, span]
                for start in range(0, rows, CHUNK):
                    chunk = slice(start, start + CHUNK)
                    e = jnp.exp2(s_ref[slot, chunk, span] * RATE - shift)
                    e_ref[slot, h, chunk] = e.astype(BF16)
                    part = part + jnp.sum(e.reshape(-1, 8, half), axis=0)
                totals.append(part)
            return jnp.concatenate(totals, axis=1)

        def attend(index):
            values = block_of(keys_ref, index, 1)
            for c in range(0, heads, GROUP):
                span = slice(c * half, (c + GROUP) * half)
                weights = wide(e_ref.at[bases[t] + index], c, GROUP)
                acc_ref[t, :, span] += dot(values, weights, 0, 0)

        def step(index, total):
            attend(index - 1)
            return weigh(index, total)

        acc_ref[t] = jnp.zeros(acc_ref.shape[1:], F32)
        total = weigh(0, jnp.zeros((8, cols), F32))
        total = lax.fori_loop(1, counts[t], step, total)
        attend(counts[t] - 1)
        results.append((shifts[t], jnp.sum(total, axis=0, keepdims=True)))
    return results


def backward(keys_ref, parity, stretches, qt_ref, gt_ref, delta_ref, e_ref, acc_ref, out_ref):
    runs, pairs, slices, _, grain, _ = keys_ref.shape
    heads = qt_ref.shape[0] // 2
    half = runs * slices * grain
    blocks = pairs // 2
    counts = counts_of(stretches, parity)

    def store(index, which, value):
        for u in range(2):
            part = value[u * half : (u + 1) * half].reshape(runs, slices, grain, HD)
            out_ref[:, 2 * index + u, :, which] = part.astype(BF16)

    def pull(index, both):
        keys = block_of(keys_ref, index, 0)
        values = block_of(keys_ref, index, 1)
        key_term = value_term = 0.0
        for t in range(2 if both else 1):
            slot = index if t == 0 else blocks + index
            for c in range(0, heads, GROUP):
                span = slice(c * half, (c + GROUP) * half)
                weights = wide(e_ref.at[slot], c, GROUP)
                grads = wide(gt_ref, t * heads + c, GROUP)
                slope = dot(values, grads, 1, 0) - delta_ref[t, :, span]
                ds = (weights.astype(F32) * slope).astype(BF16)
                value_term = value_term + dot(grads, weights, 1, 1)
                key_term = key_term + dot(wide(qt_ref, t * heads + c, GROUP), ds, 1, 1)
                acc_ref[t, :, span] += dot(keys, ds, 0, 0)
        store(index, 0, (key_term * SCALE).T)
        store(index, 1, value_term.T)

    @pl.loop(0, counts[1])
    def _(index):
        pull(index, True)

    @pl.loop(counts[1], counts[0])
    def _(index):
        pull(index, False)

    @pl.loop(counts[0], blocks)
    def _(index):
        for which in range(2):
            store(index, which, jnp.zeros((2 * half, HD), F32))


def first_kernel(order_ref, q_ref, keys_ref, qt_ref, e_ref, acc_ref, stat_ref, s_ref):
    half = q_ref.shape[0] // 2
    heads = q_ref.shape[1] // HD
    stretches, offsets = stretches_of(order_ref, half)
    for t in range(2):
        for h in range(heads):
            block = q_ref[pl.ds(offsets[t], half), h * HD : (h + 1) * HD]
            qt_ref[t * heads + h] = flip(block).astype(BF16)
    parity = lax.axis_index("core")
    results = forward(keys_ref, parity, stretches, qt_ref, s_ref, e_ref, acc_ref)
    for t in range(2):
        for k in range(2):
            stat_ref[2 * t + k] = results[t][k]


def second_kernel(
    order_ref,
    g_ref,
    keys_ref,
    qt_ref,
    old_acc_ref,
    old_stat_ref,
    out_ref,
    gt_ref,
    delta_ref,
    dkeys_ref,
    dq_acc_ref,
    s_ref,
    e_ref,
    acc_ref,
    own_gt_ref,
    own_delta_ref,
):
    half = g_ref.shape[0] // 2
    heads = g_ref.shape[1] // HD
    stretches, offsets = stretches_of(order_ref, half)
    parity = 1 - lax.axis_index("core")
    results = forward(keys_ref, parity, stretches, qt_ref, s_ref, e_ref, acc_ref)
    for t in range(2):
        old_shift, old_total = old_stat_ref[2 * t], old_stat_ref[2 * t + 1]
        new_shift, new_total = results[t]
        shift = jnp.maximum(old_shift, new_shift)
        old_part = jnp.exp2(old_shift - shift)
        new_part = jnp.exp2(new_shift - shift)
        inverse = 1.0 / (old_total * old_part + new_total * new_part)
        old_part = old_part * inverse
        new_part = new_part * inverse
        for h in range(heads):
            part = slice(h * half, (h + 1) * half)
            column = slice(h * HD, (h + 1) * HD)
            total = old_acc_ref[t, :, part] * old_part[:, part]
            total = total + acc_ref[t, :, part] * new_part[:, part]
            out = total.astype(BF16)
            out_ref[pl.ds(offsets[t], half), column] = flip(out).astype(BF16)
            grad = flip(g_ref[pl.ds(offsets[t], half), column])
            gt_ref[t * heads + h] = (grad * old_part[:, part]).astype(BF16)
            own_gt_ref[t * heads + h] = (grad * new_part[:, part]).astype(BF16)
            delta = jnp.sum(grad * out.astype(F32), axis=0, keepdims=True)
            delta_ref[t, :, part] = delta * old_part[:, part]
            own_delta_ref[t, :, part] = delta * new_part[:, part]
        dq_acc_ref[t] = jnp.zeros(dq_acc_ref.shape[1:], F32)
    backward(
        keys_ref,
        parity,
        stretches,
        qt_ref,
        own_gt_ref,
        own_delta_ref,
        e_ref,
        dq_acc_ref,
        dkeys_ref,
    )


def third_kernel(
    order_ref,
    keys_ref,
    qt_ref,
    gt_ref,
    delta_ref,
    e_ref,
    old_acc_ref,
    dkeys_ref,
    dq_ref,
    acc_ref,
):
    half = dq_ref.shape[0] // 2
    heads = dq_ref.shape[1] // HD
    stretches, offsets = stretches_of(order_ref, half)
    parity = lax.axis_index("core")
    acc_ref[...] = old_acc_ref[...]
    backward(
        keys_ref,
        parity,
        stretches,
        qt_ref,
        gt_ref,
        delta_ref,
        e_ref,
        acc_ref,
        dkeys_ref,
    )
    for t in range(2):
        for h in range(heads):
            value = (acc_ref[t, :, h * half : (h + 1) * half] * SCALE).T.astype(BF16)
            dq_ref[pl.ds(offsets[t], half), h * HD : (h + 1) * HD] = value


def call(kernel, name, outs, scratch, flops, *args):
    vmem = pl.BlockSpec(memory_space=pltpu.VMEM)
    return pl.pallas_call(
        kernel,
        out_shape=tuple(jax.ShapeDtypeStruct(*out) for out in outs),
        in_specs=[pl.BlockSpec(memory_space=pltpu.SMEM)] + [vmem] * (len(args) - 1),
        out_specs=(vmem,) * len(outs),
        scratch_shapes=[pltpu.VMEM(*item) for item in scratch],
        compiler_params=pltpu.CompilerParams(vmem_limit_bytes=VMEM_BYTES),
        cost_estimate=pl.CostEstimate(
            flops=flops, bytes_accessed=8 << 20, transcendentals=0
        ),
        name=name,
    )(*args)


def shapes_of(queries, keys):
    rows, width = queries.shape
    half = rows // 2
    cols = width // HD * half
    slots = keys.shape[1] // 2 + keys.shape[1] // 4
    heads = cols // half
    return dict(
        weights=((slots, heads, 2 * half, half), BF16),
        scores=((slots, 2 * half, cols), F32),
        flat=((2 * heads, HD, half), BF16),
        acc=((2, HD, cols), F32),
        row=((2, 1, cols), F32),
        stat=((4, 1, cols), F32),
        keys=(keys.shape, BF16),
        queries=(queries.shape, BF16),
    )


def attend_mine(order, queries, mine):
    s = shapes_of(queries, mine)
    outs = (s["flat"], s["weights"], s["acc"], s["stat"])
    return call(
        first_kernel, "first", outs, (s["scores"],), 3 << 30, order, queries, mine
    )


def attend_theirs(order, grads, theirs, qt, acc, stat):
    s = shapes_of(grads, theirs)
    outs = (s["queries"], s["flat"], s["row"], s["keys"], s["acc"])
    scratch = (s["scores"], s["weights"], s["acc"], s["flat"], s["row"])
    return call(
        second_kernel, "second", outs, scratch, 6 << 30, order, grads, theirs, qt, acc, stat
    )


def finish_mine(order, queries, mine, qt, gt, delta, weights, acc):
    s = shapes_of(queries, mine)
    outs = (s["keys"], s["queries"])
    return call(
        third_kernel,
        "third",
        outs,
        (s["acc"],),
        4 << 30,
        order,
        mine,
        qt,
        gt,
        delta,
        weights,
        acc,
    )


AXES = ("zl", "xh", "xl", "core", "y", "zh")
SPREAD = ("y", "zl", "xh", "xl", "zh")
SWAP = ((0, 1), (1, 0))


def per_device(queries, key_vectors, value_vectors, out_grads, pair_order):
    sizes = {name: lax.axis_size(name) for name in AXES}
    runs, zl, xh, xl, zh = (sizes[name] for name in SPREAD)
    rows = key_vectors.shape[0]
    kv_heads = key_vectors.shape[1] // HD
    pairs = zl * xh * xl
    block = (2, rows, HD)

    both = jnp.stack([key_vectors, value_vectors]).reshape(2, rows, kv_heads, HD)
    sent = both.transpose(2, 0, 1, 3).reshape((1, zl, xh, 1, 1) + block)
    sent = jnp.broadcast_to(sent, (runs, zl, xh, xl, zh) + block)
    sent = sent.reshape((runs * pairs * zh,) + block)
    mine = lax.all_to_all(sent, SPREAD, split_axis=0, concat_axis=0, tiled=True)
    mine = mine.reshape((runs, pairs, zh) + block)
    theirs = lax.ppermute(mine, "core", SWAP)

    qt, weights, acc, stat = attend_mine(pair_order, queries, mine)
    attended, gt, delta, dtheirs, acc = attend_theirs(
        pair_order, out_grads, theirs, qt, acc, stat
    )
    other = lax.ppermute(dtheirs, "core", SWAP)
    dmine, query_grads = finish_mine(
        pair_order, queries, mine, qt, gt, delta, weights, acc
    )
    total = (dmine.astype(F32) + other.astype(F32)).astype(BF16)
    total = total.reshape((runs * pairs * zh,) + block)
    got = lax.all_to_all(total, SPREAD, split_axis=0, concat_axis=0, tiled=True)
    got = got.reshape((runs, kv_heads, xl * zh) + block)
    total = got.astype(F32).sum(axis=(0, 2))
    total = total.transpose(1, 2, 0, 3).reshape(2, rows, kv_heads * HD)
    return attended, query_grads, total[0], total[1]


def solution(mesh):
    fine = Mesh(mesh.devices.reshape(4, 2, 2, 2, 8, 2), AXES)
    fsdp, cp = AXES[:4], AXES[4:]
    return jax.shard_map(
        per_device,
        mesh=fine,
        in_specs=(P(cp, fsdp), P(AXES, None), P(AXES, None), P(cp, fsdp), P()),
        out_specs=(P(cp, fsdp), P(cp, fsdp), P(AXES, None), P(AXES, None)),
        check_vma=False,
    )
```

```python
import math
import jax
import jax.numpy as jnp
from jax import lax
from jax.experimental import pallas as pl
from jax.experimental.pallas import tpu as pltpu
from jax.sharding import Mesh, PartitionSpec as P

HD = 128
BF16 = jnp.bfloat16
F32 = jnp.float32
SCALE = 1.0 / math.sqrt(HD)
RATE = SCALE * math.log2(math.e)
FILL = -1e30
VMEM_BYTES = 32 << 20
CHUNK = 64
GROUP = 4


def dot(a, b, a_axis, b_axis):
    return lax.dot_general(
        a, b, (((a_axis,), (b_axis,)), ((), ())), preferred_element_type=F32
    )


def flip(x):
    return x.astype(F32).T


def stretches_of(order_ref, half):
    first = 2 * (lax.axis_index("y") * lax.axis_size("zh") + lax.axis_index("zh"))
    late = jnp.where(order_ref[first + 1] > order_ref[first], 1, 0)
    stretches = (order_ref[first + late], order_ref[first + 1 - late])
    offsets = (
        pl.multiple_of(late * half, half),
        pl.multiple_of((1 - late) * half, half),
    )
    return stretches, offsets


def counts_of(stretches, parity):
    seen = [lax.shift_right_logical(s - parity + 2, 1) for s in stretches]
    return tuple(jnp.maximum(lax.shift_right_logical(n + 1, 1), 1) for n in seen)


def block_of(ref, index, which):
    runs, _, slices, _, _, grain, _ = ref.shape
    parts = [
        ref[:, index, :, u, which].astype(F32).reshape(runs * slices * grain, HD)
        for u in range(2)
    ]
    return jnp.concatenate(parts, axis=0).astype(BF16)


def wide(ref, first, count):
    return jnp.concatenate([ref[first + k] for k in range(count)], axis=1)


def forward(keys_ref, parity, stretches, qt_ref, s_ref, e_ref, acc_ref):
    rows, cols = s_ref.shape[1:]
    blocks = keys_ref.shape[1]
    half = rows // 2
    heads = cols // half
    counts = counts_of(stretches, parity)
    bases = (0, blocks)
    shifts = []
    for t in range(2):

        def score(index, peak, masked):
            keys = block_of(keys_ref, index, 0)
            peaks = []
            for c in range(0, heads, GROUP):
                span = slice(c * half, (c + GROUP) * half)
                s = dot(keys, wide(qt_ref, t * heads + c, GROUP), 1, 0)
                if masked:
                    j = lax.broadcasted_iota(jnp.int32, s.shape, 0)
                    r = lax.rem(lax.broadcasted_iota(jnp.int32, s.shape, 1), half)
                    j = j + jnp.where(j >= half, half, 0)
                    ahead = (4 * index + parity - stretches[t]) * half
                    s = jnp.where(j + ahead <= r, s, FILL)
                s_ref[bases[t] + index, :, span] = s
                high = jnp.max(s.reshape(-1, 8, GROUP * half), axis=0)
                peaks.append(jnp.maximum(peak[:, span], high))
            return jnp.concatenate(peaks, axis=1)

        last = counts[t] - 1
        peak = jnp.full((8, cols), FILL, F32)
        peak = lax.fori_loop(0, last, lambda i, p: score(i, p, False), peak)
        peak = score(last, peak, True)
        shifts.append(jnp.max(peak, axis=0, keepdims=True) * RATE)

    results = []
    for t in range(2):

        def weigh(index, total):
            slot = bases[t] + index
            totals = []
            for h in range(heads):
                span = slice(h * half, (h + 1) * half)
                shift = shifts[t][:, span]
                part = total[:, span]
                for start in range(0, rows, CHUNK):
                    chunk = slice(start, start + CHUNK)
                    e = jnp.exp2(s_ref[slot, chunk, span] * RATE - shift)
                    e_ref[slot, h, chunk] = e.astype(BF16)
                    part = part + jnp.sum(e.reshape(-1, 8, half), axis=0)
                totals.append(part)
            return jnp.concatenate(totals, axis=1)

        def attend(index):
            values = block_of(keys_ref, index, 1)
            for c in range(0, heads, GROUP):
                span = slice(c * half, (c + GROUP) * half)
                weights = wide(e_ref.at[bases[t] + index], c, GROUP)
                acc_ref[t, :, span] += dot(values, weights, 0, 0)

        def step(index, total):
            attend(index - 1)
            return weigh(index, total)

        acc_ref[t] = jnp.zeros(acc_ref.shape[1:], F32)
        total = weigh(0, jnp.zeros((8, cols), F32))
        total = lax.fori_loop(1, counts[t], step, total)
        attend(counts[t] - 1)
        results.append((shifts[t], jnp.sum(total, axis=0, keepdims=True)))
    return results


def backward(keys_ref, parity, stretches, qt_ref, gt_ref, delta_ref, e_ref, acc_ref, out_ref):
    runs, blocks, slices, _, _, grain, _ = keys_ref.shape
    heads = qt_ref.shape[0] // 2
    half = runs * slices * grain
    counts = counts_of(stretches, parity)

    def store(index, which, value):
        for u in range(2):
            part = value[u * half : (u + 1) * half].reshape(runs, slices, grain, HD)
            out_ref[:, index, :, u, which] = part.astype(BF16)

    def pull(index, both):
        keys = block_of(keys_ref, index, 0)
        values = block_of(keys_ref, index, 1)
        key_term = value_term = 0.0
        for t in range(2 if both else 1):
            slot = index if t == 0 else blocks + index
            for c in range(0, heads, GROUP):
                span = slice(c * half, (c + GROUP) * half)
                weights = wide(e_ref.at[slot], c, GROUP)
                grads = wide(gt_ref, t * heads + c, GROUP)
                slope = dot(values, grads, 1, 0) - delta_ref[t, :, span]
                ds = (weights.astype(F32) * slope).astype(BF16)
                value_term = value_term + dot(grads, weights, 1, 1)
                key_term = key_term + dot(wide(qt_ref, t * heads + c, GROUP), ds, 1, 1)
                acc_ref[t, :, span] += dot(keys, ds, 0, 0)
        store(index, 0, (key_term * SCALE).T)
        store(index, 1, value_term.T)

    @pl.loop(0, counts[1])
    def _(index):
        pull(index, True)

    @pl.loop(counts[1], counts[0])
    def _(index):
        pull(index, False)

    @pl.loop(counts[0], blocks)
    def _(index):
        for which in range(2):
            store(index, which, jnp.zeros((2 * half, HD), F32))


def first_kernel(order_ref, q_ref, keys_ref, qt_ref, e_ref, acc_ref, stat_ref, s_ref):
    half = q_ref.shape[0] // 2
    heads = q_ref.shape[1] // HD
    stretches, offsets = stretches_of(order_ref, half)
    for t in range(2):
        for h in range(heads):
            block = q_ref[pl.ds(offsets[t], half), h * HD : (h + 1) * HD]
            qt_ref[t * heads + h] = flip(block).astype(BF16)
    parity = lax.axis_index("core")
    results = forward(keys_ref, parity, stretches, qt_ref, s_ref, e_ref, acc_ref)
    for t in range(2):
        for k in range(2):
            stat_ref[2 * t + k] = results[t][k]


def second_kernel(
    order_ref,
    g_ref,
    keys_ref,
    qt_ref,
    old_acc_ref,
    old_stat_ref,
    out_ref,
    gt_ref,
    delta_ref,
    dkeys_ref,
    dq_acc_ref,
    s_ref,
    e_ref,
    acc_ref,
    own_gt_ref,
    own_delta_ref,
):
    half = g_ref.shape[0] // 2
    heads = g_ref.shape[1] // HD
    stretches, offsets = stretches_of(order_ref, half)
    parity = 1 - lax.axis_index("core")
    results = forward(keys_ref, parity, stretches, qt_ref, s_ref, e_ref, acc_ref)
    for t in range(2):
        old_shift, old_total = old_stat_ref[2 * t], old_stat_ref[2 * t + 1]
        new_shift, new_total = results[t]
        shift = jnp.maximum(old_shift, new_shift)
        old_part = jnp.exp2(old_shift - shift)
        new_part = jnp.exp2(new_shift - shift)
        inverse = 1.0 / (old_total * old_part + new_total * new_part)
        old_part = old_part * inverse
        new_part = new_part * inverse
        for h in range(heads):
            part = slice(h * half, (h + 1) * half)
            column = slice(h * HD, (h + 1) * HD)
            total = old_acc_ref[t, :, part] * old_part[:, part]
            total = total + acc_ref[t, :, part] * new_part[:, part]
            out = total.astype(BF16)
            out_ref[pl.ds(offsets[t], half), column] = flip(out).astype(BF16)
            grad = flip(g_ref[pl.ds(offsets[t], half), column])
            gt_ref[t * heads + h] = (grad * old_part[:, part]).astype(BF16)
            own_gt_ref[t * heads + h] = (grad * new_part[:, part]).astype(BF16)
            delta = jnp.sum(grad * out.astype(F32), axis=0, keepdims=True)
            delta_ref[t, :, part] = delta * old_part[:, part]
            own_delta_ref[t, :, part] = delta * new_part[:, part]
        dq_acc_ref[t] = jnp.zeros(dq_acc_ref.shape[1:], F32)
    backward(
        keys_ref,
        parity,
        stretches,
        qt_ref,
        own_gt_ref,
        own_delta_ref,
        e_ref,
        dq_acc_ref,
        dkeys_ref,
    )


def third_kernel(
    order_ref,
    keys_ref,
    qt_ref,
    gt_ref,
    delta_ref,
    e_ref,
    old_acc_ref,
    dkeys_ref,
    dq_ref,
    acc_ref,
):
    half = dq_ref.shape[0] // 2
    heads = dq_ref.shape[1] // HD
    stretches, offsets = stretches_of(order_ref, half)
    parity = lax.axis_index("core")
    acc_ref[...] = old_acc_ref[...]
    backward(
        keys_ref,
        parity,
        stretches,
        qt_ref,
        gt_ref,
        delta_ref,
        e_ref,
        acc_ref,
        dkeys_ref,
    )
    for t in range(2):
        for h in range(heads):
            value = (acc_ref[t, :, h * half : (h + 1) * half] * SCALE).T.astype(BF16)
            dq_ref[pl.ds(offsets[t], half), h * HD : (h + 1) * HD] = value


def call(kernel, name, outs, scratch, flops, *args):
    vmem = pl.BlockSpec(memory_space=pltpu.VMEM)
    return pl.pallas_call(
        kernel,
        out_shape=tuple(jax.ShapeDtypeStruct(*out) for out in outs),
        in_specs=[pl.BlockSpec(memory_space=pltpu.SMEM)] + [vmem] * (len(args) - 1),
        out_specs=(vmem,) * len(outs),
        scratch_shapes=[pltpu.VMEM(*item) for item in scratch],
        compiler_params=pltpu.CompilerParams(vmem_limit_bytes=VMEM_BYTES),
        cost_estimate=pl.CostEstimate(
            flops=flops, bytes_accessed=8 << 20, transcendentals=0
        ),
        name=name,
    )(*args)


def shapes_of(queries, keys):
    rows, width = queries.shape
    half = rows // 2
    cols = width // HD * half
    slots = keys.shape[1] + keys.shape[1] // 2
    heads = cols // half
    return dict(
        weights=((slots, heads, 2 * half, half), BF16),
        scores=((slots, 2 * half, cols), F32),
        flat=((2 * heads, HD, half), BF16),
        acc=((2, HD, cols), F32),
        row=((2, 1, cols), F32),
        stat=((4, 1, cols), F32),
        keys=(keys.shape, BF16),
        queries=(queries.shape, BF16),
    )


def attend_mine(order, queries, mine):
    s = shapes_of(queries, mine)
    outs = (s["flat"], s["weights"], s["acc"], s["stat"])
    return call(
        first_kernel, "first", outs, (s["scores"],), 3 << 30, order, queries, mine
    )


def attend_theirs(order, grads, theirs, qt, acc, stat):
    s = shapes_of(grads, theirs)
    outs = (s["queries"], s["flat"], s["row"], s["keys"], s["acc"])
    scratch = (s["scores"], s["weights"], s["acc"], s["flat"], s["row"])
    return call(
        second_kernel, "second", outs, scratch, 6 << 30, order, grads, theirs, qt, acc, stat
    )


def finish_mine(order, queries, mine, qt, gt, delta, weights, acc):
    s = shapes_of(queries, mine)
    outs = (s["keys"], s["queries"])
    return call(
        third_kernel,
        "third",
        outs,
        (s["acc"],),
        4 << 30,
        order,
        mine,
        qt,
        gt,
        delta,
        weights,
        acc,
    )


AXES = ("zl", "xh", "xl", "core", "y", "zh")
SPREAD = ("y", "zl", "xh", "zh")
SWAP = ((0, 1), (1, 0))


def per_device(queries, key_vectors, value_vectors, out_grads, pair_order):
    sizes = {name: lax.axis_size(name) for name in AXES}
    runs, zl, xh, zh = (sizes[name] for name in SPREAD)
    rows = key_vectors.shape[0]
    kv_heads = key_vectors.shape[1] // HD
    block = (2, rows, HD)
    right = lax.axis_index("xl") == 1

    both = jnp.stack([key_vectors, value_vectors]).reshape(2, rows, kv_heads, HD)
    both = both.transpose(2, 0, 1, 3)
    near = lax.ppermute(both, "xl", SWAP)
    sent = jnp.stack([jnp.where(right, near, both), jnp.where(right, both, near)], 1)
    sent = sent.reshape((1, zl * xh, 1, 2) + block)
    sent = jnp.broadcast_to(sent, (runs, zl * xh, zh, 2) + block)
    sent = sent.reshape((runs * zl * xh * zh, 2) + block)
    mine = lax.all_to_all(sent, SPREAD, split_axis=0, concat_axis=0, tiled=True)
    mine = mine.reshape((runs, zl * xh, zh, 2) + block)
    theirs = lax.ppermute(mine, "core", SWAP)

    qt, weights, acc, stat = attend_mine(pair_order, queries, mine)
    attended, gt, delta, dtheirs, acc = attend_theirs(
        pair_order, out_grads, theirs, qt, acc, stat
    )
    other = lax.ppermute(dtheirs, "core", SWAP)
    dmine, query_grads = finish_mine(
        pair_order, queries, mine, qt, gt, delta, weights, acc
    )
    total = (dmine.astype(F32) + other.astype(F32)).astype(BF16)
    total = total.reshape((runs * zl * xh * zh, 2) + block)
    got = lax.all_to_all(total, SPREAD, split_axis=0, concat_axis=0, tiled=True)
    got = got.reshape((runs, kv_heads, zh, 2) + block)
    total = got.astype(F32).sum(axis=(0, 2))
    own = jnp.where(right, total[:, 1], total[:, 0])
    away = jnp.where(right, total[:, 0], total[:, 1]).astype(BF16)
    total = own + lax.ppermute(away, "xl", SWAP).astype(F32)
    total = total.transpose(1, 2, 0, 3).reshape(2, rows, kv_heads * HD)
    return attended, query_grads, total[0], total[1]


def solution(mesh):
    fine = Mesh(mesh.devices.reshape(4, 2, 2, 2, 8, 2), AXES)
    fsdp, cp = AXES[:4], AXES[4:]
    return jax.shard_map(
        per_device,
        mesh=fine,
        in_specs=(P(cp, fsdp), P(AXES, None), P(AXES, None), P(cp, fsdp), P()),
        out_specs=(P(cp, fsdp), P(cp, fsdp), P(AXES, None), P(AXES, None)),
        check_vma=False,
    )
```

```python
import math
import jax
import jax.numpy as jnp
from jax import lax
from jax.experimental import pallas as pl
from jax.experimental.pallas import tpu as pltpu
from jax.sharding import Mesh, PartitionSpec as P


HD = 128
BF16 = jnp.bfloat16
F32 = jnp.float32
SCALE = 1.0 / math.sqrt(HD)
RATE = SCALE * math.log2(math.e)
FILL = -1e30
VMEM_BYTES = 24 << 20
CHUNK = 64
GROUP = 4
EXTRA = 16


def dot(a, b, a_axis, b_axis):
    return lax.dot_general(
        a, b, (((a_axis,), (b_axis,)), ((), ())), preferred_element_type=F32
    )


def flip(x):
    return x.astype(F32).T


def stretches_of(order_ref, half):
    first = 2 * (lax.axis_index("y") * lax.axis_size("zh") + lax.axis_index("zh"))
    late = jnp.where(order_ref[first + 1] > order_ref[first], 1, 0)
    stretches = (order_ref[first + late], order_ref[first + 1 - late])
    offsets = (
        pl.multiple_of(late * half, half),
        pl.multiple_of((1 - late) * half, half),
    )
    return stretches, offsets


def counts_of(stretches, parity):
    seen = [lax.shift_right_logical(s - parity + 2, 1) for s in stretches]
    return tuple(jnp.maximum(lax.shift_right_logical(n + 1, 1), 1) for n in seen)


def block_of(ref, index, which):
    runs, _, slices, _, grain, _ = ref.shape
    parts = [
        ref[:, 2 * index + u, :, which].astype(F32).reshape(runs * slices * grain, HD)
        for u in range(2)
    ]
    return jnp.concatenate(parts, axis=0).astype(BF16)


def wide(ref, first, count):
    return jnp.concatenate([ref[first + k] for k in range(count)], axis=1)


def forward(keys_ref, parity, stretches, qt_ref, s_ref, e_ref, acc_ref):
    rows, cols = s_ref.shape[1:]
    blocks = keys_ref.shape[1] // 2
    half = rows // 2
    heads = cols // half
    counts = counts_of(stretches, parity)
    bases = (0, blocks)
    shifts = []
    for t in range(2):

        def score(index, peak, masked):
            keys = block_of(keys_ref, index, 0)
            peaks = []
            for c in range(0, heads, GROUP):
                span = slice(c * half, (c + GROUP) * half)
                s = dot(keys, wide(qt_ref, t * heads + c, GROUP), 1, 0)
                if masked:
                    j = lax.broadcasted_iota(jnp.int32, s.shape, 0)
                    r = lax.rem(lax.broadcasted_iota(jnp.int32, s.shape, 1), half)
                    j = j + jnp.where(j >= half, half, 0)
                    ahead = (4 * index + parity - stretches[t]) * half
                    s = jnp.where(j + ahead <= r, s, FILL)
                s = s * RATE
                s_ref[bases[t] + index, :, span] = s
                high = jnp.max(s.reshape(-1, 8, GROUP * half), axis=0)
                peaks.append(jnp.maximum(peak[:, span], high))
            return jnp.concatenate(peaks, axis=1)

        last = counts[t] - 1
        peak = jnp.full((8, cols), FILL, F32)
        peak = lax.fori_loop(0, last, lambda i, p: score(i, p, False), peak)
        peak = score(last, peak, True)
        shifts.append(jnp.max(peak, axis=0, keepdims=True))

    results = []
    for t in range(2):

        def weigh(index):
            slot = bases[t] + index
            for h in range(heads):
                span = slice(h * half, (h + 1) * half)
                shift = shifts[t][:, span]
                for start in range(0, rows, CHUNK):
                    chunk = slice(start, start + CHUNK)
                    e = jnp.exp2(s_ref[slot, chunk, span] - shift)
                    e_ref[slot, h, chunk] = e.astype(BF16)

        def attend(index):
            values = block_of(keys_ref, index, 1).T
            ones = jnp.ones((EXTRA, rows), BF16)
            lines = jnp.concatenate([values, ones], axis=0)
            weights = wide(e_ref.at[bases[t] + index], 0, heads)
            acc_ref[t] += dot(lines, weights, 1, 0)

        acc_ref[t] = jnp.zeros(acc_ref.shape[1:], F32)
        weigh(0)

        @pl.loop(1, counts[t])
        def _(index):
            attend(index - 1)
            weigh(index)

        attend(counts[t] - 1)
        results.append((shifts[t], acc_ref[t, HD : HD + 1]))
    return results


def backward(keys_ref, parity, stretches, qt_ref, gt_ref, delta_ref, e_ref, out_ref):
    runs, pairs, slices, _, grain, _ = keys_ref.shape
    heads = qt_ref.shape[0] // 2
    half = runs * slices * grain
    blocks = pairs // 2
    counts = counts_of(stretches, parity)

    def store(index, which, value):
        for u in range(2):
            part = value[u * half : (u + 1) * half].reshape(runs, slices, grain, HD)
            out_ref[:, 2 * index + u, :, which] = part.astype(BF16)

    def pull(index, both):
        values = block_of(keys_ref, index, 1)
        key_term = value_term = 0.0
        for t in range(2 if both else 1):
            slot = index if t == 0 else blocks + index
            weights = wide(e_ref.at[slot], 0, heads)
            grads = wide(gt_ref, t * heads, heads)
            slope = dot(values, grads, 1, 0)
            parts = []
            for h in range(heads):
                span = slice(h * half, (h + 1) * half)
                part = e_ref[slot, h].astype(F32) * (slope[:, span] - delta_ref[t, :, span])
                parts.append(part.astype(BF16))
            ds = jnp.concatenate(parts, axis=1)
            value_term = value_term + dot(grads, weights, 1, 1)
            key_term = key_term + dot(wide(qt_ref, t * heads, heads), ds, 1, 1)
        store(index, 0, (key_term * SCALE).T)
        store(index, 1, value_term.T)

    @pl.loop(0, counts[1])
    def _(index):
        pull(index, True)

    @pl.loop(counts[1], counts[0])
    def _(index):
        pull(index, False)

    @pl.loop(counts[0], blocks)
    def _(index):
        for which in range(2):
            store(index, which, jnp.zeros((2 * half, HD), F32))


def prepare_kernel(order_ref, q_ref, g_ref, qt_ref, gt_ref):
    half = q_ref.shape[0] // 2
    heads = q_ref.shape[1] // HD
    _, offsets = stretches_of(order_ref, half)
    for t in range(2):
        for h in range(heads):
            rows, column = pl.ds(offsets[t], half), slice(h * HD, (h + 1) * HD)
            qt_ref[t * heads + h] = flip(q_ref[rows, column]).astype(BF16)
            gt_ref[t * heads + h] = flip(g_ref[rows, column]).astype(BF16)


def first_kernel(order_ref, keys_ref, qt_ref, e_ref, acc_ref, stat_ref, s_ref):
    stretches, _ = stretches_of(order_ref, s_ref.shape[1] // 2)
    parity = lax.axis_index("core")
    results = forward(keys_ref, parity, stretches, qt_ref, s_ref, e_ref, acc_ref)
    for t in range(2):
        for k in range(2):
            stat_ref[2 * t + k] = results[t][k]


def second_kernel(
    order_ref,
    keys_ref,
    qt_ref,
    g_ref,
    old_acc_ref,
    old_stat_ref,
    out_ref,
    gt_ref,
    delta_ref,
    own_gt_ref,
    own_delta_ref,
    shift_ref,
    dkeys_ref,
    s_ref,
    e_ref,
    acc_ref,
):
    half = s_ref.shape[1] // 2
    heads = g_ref.shape[0] // 2
    stretches, _ = stretches_of(order_ref, half)
    parity = 1 - lax.axis_index("core")
    results = forward(keys_ref, parity, stretches, qt_ref, s_ref, e_ref, acc_ref)
    for t in range(2):
        old_shift, old_total = old_stat_ref[2 * t], old_stat_ref[2 * t + 1]
        new_shift, new_total = results[t]
        shift_ref[t] = new_shift
        shift = jnp.maximum(old_shift, new_shift)
        old_part = jnp.exp2(old_shift - shift)
        new_part = jnp.exp2(new_shift - shift)
        inverse = 1.0 / (old_total * old_part + new_total * new_part)
        old_part = old_part * inverse
        new_part = new_part * inverse
        for h in range(heads):
            part = slice(h * half, (h + 1) * half)
            panel = t * heads + h
            total = old_acc_ref[t, :HD, part] * old_part[:, part]
            total = total + acc_ref[t, :HD, part] * new_part[:, part]
            out = total.astype(BF16)
            out_ref[panel] = out
            grad = g_ref[panel].astype(F32)
            gt_ref[panel] = (grad * old_part[:, part]).astype(BF16)
            own_gt_ref[panel] = (grad * new_part[:, part]).astype(BF16)
            delta = jnp.sum(grad * out.astype(F32), axis=0, keepdims=True)
            delta_ref[t, :, part] = delta * old_part[:, part]
            own_delta_ref[t, :, part] = delta * new_part[:, part]
    backward(
        keys_ref,
        parity,
        stretches,
        qt_ref,
        own_gt_ref,
        own_delta_ref,
        e_ref,
        dkeys_ref,
    )


def third_kernel(order_ref, keys_ref, qt_ref, gt_ref, delta_ref, e_ref, dkeys_ref):
    stretches, _ = stretches_of(order_ref, e_ref.shape[2] // 2)
    parity = lax.axis_index("core")
    backward(
        keys_ref, parity, stretches, qt_ref, gt_ref, delta_ref, e_ref, dkeys_ref
    )


def last_kernel(
    order_ref,
    mine_ref,
    theirs_ref,
    qt_ref,
    gt_ref,
    own_gt_ref,
    delta_ref,
    own_delta_ref,
    stat_ref,
    shift_ref,
    out_t_ref,
    out_ref,
    dq_ref,
    acc_ref,
):
    half = dq_ref.shape[0] // 2
    heads = dq_ref.shape[1] // HD
    stretches, offsets = stretches_of(order_ref, half)
    core = lax.axis_index("core")
    acc_ref[...] = jnp.zeros(acc_ref.shape, F32)

    def add(t, keys_ref, parity, panels_ref, row_ref, shift, index):
        keys = block_of(keys_ref, index, 0)
        values = block_of(keys_ref, index, 1)
        s = dot(keys, wide(qt_ref, t * heads, heads), 1, 0)
        j = lax.broadcasted_iota(jnp.int32, s.shape, 0)
        r = lax.rem(lax.broadcasted_iota(jnp.int32, s.shape, 1), half)
        j = j + jnp.where(j >= half, half, 0)
        ahead = (4 * index + parity - stretches[t]) * half
        s = jnp.where(j + ahead <= r, s, FILL) * RATE
        e = jnp.exp2(s - shift).astype(BF16).astype(F32)
        slope = dot(values, wide(panels_ref, t * heads, heads), 1, 0) - row_ref[t]
        acc_ref[t] += dot(keys, (e * slope).astype(BF16), 0, 0)

    for t in range(2):
        shift = stat_ref[2 * t]

        @pl.loop(0, counts_of(stretches, core)[t])
        def _(index, t=t, shift=shift):
            add(t, mine_ref, core, gt_ref, delta_ref, shift, index)

        shift = shift_ref[t]

        @pl.loop(0, counts_of(stretches, 1 - core)[t])
        def _(index, t=t, shift=shift):
            add(t, theirs_ref, 1 - core, own_gt_ref, own_delta_ref, shift, index)

    for t in range(2):
        for h in range(heads):
            rows, column = pl.ds(offsets[t], half), slice(h * HD, (h + 1) * HD)
            value = acc_ref[t, :, h * half : (h + 1) * half] * SCALE
            dq_ref[rows, column] = value.T.astype(BF16)
            out_ref[rows, column] = flip(out_t_ref[t * heads + h]).astype(BF16)


def call(kernel, outs, scratch, flops, *args):
    vmem = pl.BlockSpec(memory_space=pltpu.VMEM)
    return pl.pallas_call(
        kernel,
        out_shape=tuple(jax.ShapeDtypeStruct(*out) for out in outs),
        in_specs=[pl.BlockSpec(memory_space=pltpu.SMEM)] + [vmem] * (len(args) - 1),
        out_specs=(vmem,) * len(outs),
        scratch_shapes=[pltpu.VMEM(*item) for item in scratch],
        compiler_params=pltpu.CompilerParams(vmem_limit_bytes=VMEM_BYTES),
        cost_estimate=pl.CostEstimate(
            flops=flops, bytes_accessed=8 << 20, transcendentals=0
        ),
    )(*args)


def shapes_of(queries, keys):
    rows, width = queries.shape
    half = rows // 2
    cols = width // HD * half
    slots = keys.shape[1] // 2 + keys.shape[1] // 4
    heads = cols // half
    return dict(
        weights=((slots, heads, 2 * half, half), BF16),
        scores=((slots, 2 * half, cols), F32),
        flat=((2 * heads, HD, half), BF16),
        acc=((2, HD, cols), F32),
        sums=((2, HD + EXTRA, cols), F32),
        row=((2, 1, cols), F32),
        stat=((4, 1, cols), F32),
        keys=(keys.shape, BF16),
        queries=(queries.shape, BF16),
    )


def prepare(order, queries, grads, keys):
    s = shapes_of(queries, keys)
    outs = (s["flat"], s["flat"])
    return call(prepare_kernel, outs, (), 1 << 28, order, queries, grads)


def attend_mine(order, queries, mine, qt):
    s = shapes_of(queries, mine)
    outs = (s["weights"], s["sums"], s["stat"])
    return call(first_kernel, outs, (s["scores"],), 3 << 30, order, mine, qt)


def attend_theirs(order, queries, theirs, qt, grads, acc, stat):
    s = shapes_of(queries, theirs)
    outs = (s["flat"], s["flat"], s["row"], s["flat"], s["row"], s["row"], s["keys"])
    scratch = (s["scores"], s["weights"], s["sums"])
    return call(
        second_kernel, outs, scratch, 6 << 30, order, theirs, qt, grads, acc, stat
    )


def finish_mine(order, queries, mine, qt, gt, delta, weights):
    s = shapes_of(queries, mine)
    outs = (s["keys"],)
    args = (order, mine, qt, gt, delta, weights)
    return call(third_kernel, outs, (), 4 << 30, *args)[0]


def finish_queries(order, queries, mine, *args):
    s = shapes_of(queries, mine)
    outs = (s["queries"], s["queries"])
    scratch = (s["acc"],)
    return call(last_kernel, outs, scratch, 6 << 30, order, mine, *args)


AXES = ("zl", "xh", "xl", "core", "y", "zh")
SPREAD = ("y", "zl", "xh", "xl", "zh")
SWAP = ((0, 1), (1, 0))


def per_device(queries, key_vectors, value_vectors, out_grads, pair_order):
    sizes = {name: lax.axis_size(name) for name in AXES}
    runs, zl, xh, xl, zh = (sizes[name] for name in SPREAD)
    rows = key_vectors.shape[0]
    kv_heads = key_vectors.shape[1] // HD
    pairs = zl * xh * xl
    block = (2, rows, HD)

    both = jnp.stack([key_vectors, value_vectors]).reshape(2, rows, kv_heads, HD)
    sent = both.transpose(2, 0, 1, 3).reshape((1, zl, xh, 1, 1) + block)
    sent = jnp.broadcast_to(sent, (runs, zl, xh, xl, zh) + block)
    sent = sent.reshape((runs * pairs * zh,) + block)
    mine = lax.all_to_all(sent, SPREAD, split_axis=0, concat_axis=0, tiled=True)
    shape = jax.ShapeDtypeStruct((runs, pairs, zh) + block, BF16)
    qt, grads = prepare(pair_order, queries, out_grads, shape)
    mine = mine.reshape((runs, pairs, zh) + block)
    theirs = lax.ppermute(mine, "core", SWAP)

    weights, acc, stat = attend_mine(pair_order, queries, mine, qt)
    out_t, gt, delta, own_gt, own_delta, shift, dtheirs = attend_theirs(
        pair_order, queries, theirs, qt, grads, acc, stat
    )
    other = lax.ppermute(dtheirs, "core", SWAP)
    dmine = finish_mine(pair_order, queries, mine, qt, gt, delta, weights)
    total = (dmine.astype(F32) + other.astype(F32)).astype(BF16)
    total = total.reshape((runs * pairs * zh,) + block)
    got = lax.all_to_all(total, SPREAD, split_axis=0, concat_axis=0, tiled=True)
    got = got.reshape((runs, kv_heads, xl * zh) + block)
    total = got.astype(F32).sum(axis=(0, 2))
    total = total.transpose(1, 2, 0, 3).reshape(2, rows, kv_heads * HD)
    panels = (qt, gt, own_gt, delta, own_delta, stat, shift, out_t)
    attended, query_grads = finish_queries(pair_order, queries, mine, theirs, *panels)
    return attended, query_grads, total[0], total[1]


def solution(mesh):
    fine = Mesh(mesh.devices.reshape(4, 2, 2, 2, 8, 2), AXES)
    fsdp, cp = AXES[:4], AXES[4:]
    return jax.shard_map(
        per_device,
        mesh=fine,
        in_specs=(P(cp, fsdp), P(AXES, None), P(AXES, None), P(cp, fsdp), P()),
        out_specs=(P(cp, fsdp), P(cp, fsdp), P(AXES, None), P(AXES, None)),
        check_vma=False,
    )
```

```python
import math
import jax
import jax.numpy as jnp
from jax import lax
from jax.experimental import pallas as pl
from jax.experimental.pallas import tpu as pltpu
from jax.sharding import Mesh, PartitionSpec as P

HD = 128
BF16 = jnp.bfloat16
F32 = jnp.float32
SCALE = 1.0 / math.sqrt(HD)
RATE = SCALE * math.log2(math.e)
FILL = -1e30
VMEM_BYTES = 32 << 20
CHUNK = 64
GROUP = 4
EXTRA = 16


def dot(a, b, a_axis, b_axis):
    return lax.dot_general(
        a, b, (((a_axis,), (b_axis,)), ((), ())), preferred_element_type=F32
    )


def flip(x):
    return x.astype(F32).T


def stretches_of(order_ref, half):
    first = 2 * (lax.axis_index("y") * lax.axis_size("zh") + lax.axis_index("zh"))
    late = jnp.where(order_ref[first + 1] > order_ref[first], 1, 0)
    stretches = (order_ref[first + late], order_ref[first + 1 - late])
    offsets = (
        pl.multiple_of(late * half, half),
        pl.multiple_of((1 - late) * half, half),
    )
    return stretches, offsets


def counts_of(stretches, parity):
    seen = [lax.shift_right_logical(s - parity + 2, 1) for s in stretches]
    return tuple(jnp.maximum(lax.shift_right_logical(n + 1, 1), 1) for n in seen)


def block_of(ref, index, which):
    runs, _, slices, _, grain, _ = ref.shape
    parts = [
        ref[:, 2 * index + u, :, which].astype(F32).reshape(runs * slices * grain, HD)
        for u in range(2)
    ]
    return jnp.concatenate(parts, axis=0).astype(BF16)


def wide(ref, first, count):
    return jnp.concatenate([ref[first + k] for k in range(count)], axis=1)


def forward(keys_ref, parity, stretches, qt_ref, s_ref, e_ref, acc_ref):
    rows, cols = s_ref.shape[1:]
    blocks = keys_ref.shape[1] // 2
    half = rows // 2
    heads = cols // half
    counts = counts_of(stretches, parity)
    bases = (0, blocks)
    shifts = []
    for t in range(2):

        def score(index, peak, masked):
            keys = block_of(keys_ref, index, 0)
            peaks = []
            for c in range(0, heads, GROUP):
                span = slice(c * half, (c + GROUP) * half)
                s = dot(keys, wide(qt_ref, t * heads + c, GROUP), 1, 0)
                if masked:
                    j = lax.broadcasted_iota(jnp.int32, s.shape, 0)
                    r = lax.rem(lax.broadcasted_iota(jnp.int32, s.shape, 1), half)
                    j = j + jnp.where(j >= half, half, 0)
                    ahead = (4 * index + parity - stretches[t]) * half
                    s = jnp.where(j + ahead <= r, s, FILL)
                s = s * RATE
                s_ref[bases[t] + index, :, span] = s
                high = jnp.max(s.reshape(-1, 8, GROUP * half), axis=0)
                peaks.append(jnp.maximum(peak[:, span], high))
            return jnp.concatenate(peaks, axis=1)

        last = counts[t] - 1
        peak = jnp.full((8, cols), FILL, F32)
        peak = lax.fori_loop(0, last, lambda i, p: score(i, p, False), peak)
        peak = score(last, peak, True)
        shifts.append(jnp.max(peak, axis=0, keepdims=True))

    results = []
    for t in range(2):

        def weigh(index):
            slot = bases[t] + index
            for h in range(heads):
                span = slice(h * half, (h + 1) * half)
                shift = shifts[t][:, span]
                for start in range(0, rows, CHUNK):
                    chunk = slice(start, start + CHUNK)
                    e = jnp.exp2(s_ref[slot, chunk, span] - shift)
                    e_ref[slot, h, chunk] = e.astype(BF16)

        def attend(index):
            values = block_of(keys_ref, index, 1).T
            ones = jnp.ones((EXTRA, rows), BF16)
            lines = jnp.concatenate([values, ones], axis=0)
            weights = wide(e_ref.at[bases[t] + index], 0, heads)
            acc_ref[t] += dot(lines, weights, 1, 0)

        acc_ref[t] = jnp.zeros(acc_ref.shape[1:], F32)
        weigh(0)

        @pl.loop(1, counts[t])
        def _(index):
            attend(index - 1)
            weigh(index)

        attend(counts[t] - 1)
        results.append((shifts[t], acc_ref[t, HD : HD + 1]))
    return results


def backward(keys_ref, parity, stretches, qt_ref, gt_ref, delta_ref, e_ref, acc_ref, out_ref):
    runs, pairs, slices, _, grain, _ = keys_ref.shape
    heads = qt_ref.shape[0] // 2
    half = runs * slices * grain
    blocks = pairs // 2
    counts = counts_of(stretches, parity)

    def store(index, which, value):
        for u in range(2):
            part = value[u * half : (u + 1) * half].reshape(runs, slices, grain, HD)
            out_ref[:, 2 * index + u, :, which] = part.astype(BF16)

    def pull(index, both):
        keys = block_of(keys_ref, index, 0)
        values = block_of(keys_ref, index, 1)
        key_term = value_term = 0.0
        for t in range(2 if both else 1):
            slot = index if t == 0 else blocks + index
            for c in range(0, heads, GROUP):
                span = slice(c * half, (c + GROUP) * half)
                weights = wide(e_ref.at[slot], c, GROUP)
                grads = wide(gt_ref, t * heads + c, GROUP)
                slope = dot(values, grads, 1, 0) - delta_ref[t, :, span]
                ds = (weights.astype(F32) * slope).astype(BF16)
                value_term = value_term + dot(grads, weights, 1, 1)
                key_term = key_term + dot(wide(qt_ref, t * heads + c, GROUP), ds, 1, 1)
                acc_ref[t, :, span] += dot(keys, ds, 0, 0)
        store(index, 0, (key_term * SCALE).T)
        store(index, 1, value_term.T)

    @pl.loop(0, counts[1])
    def _(index):
        pull(index, True)

    @pl.loop(counts[1], counts[0])
    def _(index):
        pull(index, False)

    @pl.loop(counts[0], blocks)
    def _(index):
        for which in range(2):
            store(index, which, jnp.zeros((2 * half, HD), F32))


def first_kernel(order_ref, q_ref, keys_ref, qt_ref, e_ref, acc_ref, stat_ref, s_ref):
    half = q_ref.shape[0] // 2
    heads = q_ref.shape[1] // HD
    stretches, offsets = stretches_of(order_ref, half)
    for t in range(2):
        for h in range(heads):
            block = q_ref[pl.ds(offsets[t], half), h * HD : (h + 1) * HD]
            qt_ref[t * heads + h] = flip(block).astype(BF16)
    parity = lax.axis_index("core")
    results = forward(keys_ref, parity, stretches, qt_ref, s_ref, e_ref, acc_ref)
    for t in range(2):
        for k in range(2):
            stat_ref[2 * t + k] = results[t][k]


def second_kernel(
    order_ref,
    g_ref,
    keys_ref,
    qt_ref,
    old_acc_ref,
    old_stat_ref,
    out_ref,
    gt_ref,
    delta_ref,
    dkeys_ref,
    dq_acc_ref,
    s_ref,
    e_ref,
    acc_ref,
    own_gt_ref,
    own_delta_ref,
):
    half = g_ref.shape[0] // 2
    heads = g_ref.shape[1] // HD
    stretches, offsets = stretches_of(order_ref, half)
    parity = 1 - lax.axis_index("core")
    results = forward(keys_ref, parity, stretches, qt_ref, s_ref, e_ref, acc_ref)
    for t in range(2):
        old_shift, old_total = old_stat_ref[2 * t], old_stat_ref[2 * t + 1]
        new_shift, new_total = results[t]
        shift = jnp.maximum(old_shift, new_shift)
        old_part = jnp.exp2(old_shift - shift)
        new_part = jnp.exp2(new_shift - shift)
        inverse = 1.0 / (old_total * old_part + new_total * new_part)
        old_part = old_part * inverse
        new_part = new_part * inverse
        for h in range(heads):
            part = slice(h * half, (h + 1) * half)
            column = slice(h * HD, (h + 1) * HD)
            total = old_acc_ref[t, :HD, part] * old_part[:, part]
            total = total + acc_ref[t, :HD, part] * new_part[:, part]
            out = total.astype(BF16)
            out_ref[pl.ds(offsets[t], half), column] = flip(out).astype(BF16)
            grad = flip(g_ref[pl.ds(offsets[t], half), column])
            gt_ref[t * heads + h] = (grad * old_part[:, part]).astype(BF16)
            own_gt_ref[t * heads + h] = (grad * new_part[:, part]).astype(BF16)
            delta = jnp.sum(grad * out.astype(F32), axis=0, keepdims=True)
            delta_ref[t, :, part] = delta * old_part[:, part]
            own_delta_ref[t, :, part] = delta * new_part[:, part]
        dq_acc_ref[t] = jnp.zeros(dq_acc_ref.shape[1:], F32)
    backward(
        keys_ref,
        parity,
        stretches,
        qt_ref,
        own_gt_ref,
        own_delta_ref,
        e_ref,
        dq_acc_ref,
        dkeys_ref,
    )


def third_kernel(
    order_ref,
    keys_ref,
    qt_ref,
    gt_ref,
    delta_ref,
    e_ref,
    old_acc_ref,
    dkeys_ref,
    dq_ref,
    acc_ref,
):
    half = dq_ref.shape[0] // 2
    heads = dq_ref.shape[1] // HD
    stretches, offsets = stretches_of(order_ref, half)
    parity = lax.axis_index("core")
    acc_ref[...] = old_acc_ref[...]
    backward(
        keys_ref,
        parity,
        stretches,
        qt_ref,
        gt_ref,
        delta_ref,
        e_ref,
        acc_ref,
        dkeys_ref,
    )
    for t in range(2):
        for h in range(heads):
            value = (acc_ref[t, :, h * half : (h + 1) * half] * SCALE).T.astype(BF16)
            dq_ref[pl.ds(offsets[t], half), h * HD : (h + 1) * HD] = value


def call(kernel, name, outs, scratch, flops, *args):
    vmem = pl.BlockSpec(memory_space=pltpu.VMEM)
    return pl.pallas_call(
        kernel,
        out_shape=tuple(jax.ShapeDtypeStruct(*out) for out in outs),
        in_specs=[pl.BlockSpec(memory_space=pltpu.SMEM)] + [vmem] * (len(args) - 1),
        out_specs=(vmem,) * len(outs),
        scratch_shapes=[pltpu.VMEM(*item) for item in scratch],
        compiler_params=pltpu.CompilerParams(vmem_limit_bytes=VMEM_BYTES),
        cost_estimate=pl.CostEstimate(
            flops=flops, bytes_accessed=8 << 20, transcendentals=0
        ),
        name=name,
    )(*args)


def shapes_of(queries, keys):
    rows, width = queries.shape
    half = rows // 2
    cols = width // HD * half
    slots = keys.shape[1] // 2 + keys.shape[1] // 4
    heads = cols // half
    return dict(
        weights=((slots, heads, 2 * half, half), BF16),
        scores=((slots, 2 * half, cols), F32),
        flat=((2 * heads, HD, half), BF16),
        acc=((2, HD, cols), F32),
        sums=((2, HD + EXTRA, cols), F32),
        row=((2, 1, cols), F32),
        stat=((4, 1, cols), F32),
        keys=(keys.shape, BF16),
        queries=(queries.shape, BF16),
    )


def attend_mine(order, queries, mine):
    s = shapes_of(queries, mine)
    outs = (s["flat"], s["weights"], s["sums"], s["stat"])
    return call(
        first_kernel, "first", outs, (s["scores"],), 3 << 30, order, queries, mine
    )


def attend_theirs(order, grads, theirs, qt, acc, stat):
    s = shapes_of(grads, theirs)
    outs = (s["queries"], s["flat"], s["row"], s["keys"], s["acc"])
    scratch = (s["scores"], s["weights"], s["sums"], s["flat"], s["row"])
    return call(
        second_kernel, "second", outs, scratch, 6 << 30, order, grads, theirs, qt, acc, stat
    )


def finish_mine(order, queries, mine, qt, gt, delta, weights, acc):
    s = shapes_of(queries, mine)
    outs = (s["keys"], s["queries"])
    return call(
        third_kernel,
        "third",
        outs,
        (s["acc"],),
        4 << 30,
        order,
        mine,
        qt,
        gt,
        delta,
        weights,
        acc,
    )


AXES = ("zl", "xh", "xl", "core", "y", "zh")
SPREAD = ("y", "zl", "xh", "xl", "zh")
SWAP = ((0, 1), (1, 0))


def per_device(queries, key_vectors, value_vectors, out_grads, pair_order):
    sizes = {name: lax.axis_size(name) for name in AXES}
    runs, zl, xh, xl, zh = (sizes[name] for name in SPREAD)
    rows = key_vectors.shape[0]
    kv_heads = key_vectors.shape[1] // HD
    pairs = zl * xh * xl
    block = (2, rows, HD)

    both = jnp.stack([key_vectors, value_vectors]).reshape(2, rows, kv_heads, HD)
    sent = both.transpose(2, 0, 1, 3).reshape((1, zl, xh, 1, 1) + block)
    sent = jnp.broadcast_to(sent, (runs, zl, xh, xl, zh) + block)
    sent = sent.reshape((runs * pairs * zh,) + block)
    mine = lax.all_to_all(sent, SPREAD, split_axis=0, concat_axis=0, tiled=True)
    mine = mine.reshape((runs, pairs, zh) + block)
    theirs = lax.ppermute(mine, "core", SWAP)

    qt, weights, acc, stat = attend_mine(pair_order, queries, mine)
    attended, gt, delta, dtheirs, acc = attend_theirs(
        pair_order, out_grads, theirs, qt, acc, stat
    )
    other = lax.ppermute(dtheirs, "core", SWAP)
    dmine, query_grads = finish_mine(
        pair_order, queries, mine, qt, gt, delta, weights, acc
    )
    total = (dmine.astype(F32) + other.astype(F32)).astype(BF16)
    total = total.reshape((runs * pairs * zh,) + block)
    got = lax.all_to_all(total, SPREAD, split_axis=0, concat_axis=0, tiled=True)
    got = got.reshape((runs, kv_heads, xl * zh) + block)
    total = got.astype(F32).sum(axis=(0, 2))
    total = total.transpose(1, 2, 0, 3).reshape(2, rows, kv_heads * HD)
    return attended, query_grads, total[0], total[1]


def solution(mesh):
    fine = Mesh(mesh.devices.reshape(4, 2, 2, 2, 8, 2), AXES)
    fsdp, cp = AXES[:4], AXES[4:]
    return jax.shard_map(
        per_device,
        mesh=fine,
        in_specs=(P(cp, fsdp), P(AXES, None), P(AXES, None), P(cp, fsdp), P()),
        out_specs=(P(cp, fsdp), P(cp, fsdp), P(AXES, None), P(AXES, None)),
        check_vma=False,
    )
```

```python
import math
import jax
import jax.numpy as jnp
from jax import lax
from jax.experimental import pallas as pl
from jax.experimental.pallas import tpu as pltpu
from jax.sharding import Mesh, PartitionSpec as P

HD = 128
BF16 = jnp.bfloat16
F32 = jnp.float32
SCALE = 1.0 / math.sqrt(HD)
RATE = SCALE * math.log2(math.e)
FILL = -1e30
VMEM_BYTES = 32 << 20
CHUNK = 64
GROUP = 4


def dot(a, b, a_axis, b_axis):
    return lax.dot_general(
        a, b, (((a_axis,), (b_axis,)), ((), ())), preferred_element_type=F32
    )


def flip(x):
    return x.astype(F32).T


def stretches_of(order_ref, half):
    first = 2 * (lax.axis_index("y") * lax.axis_size("zh") + lax.axis_index("zh"))
    late = jnp.where(order_ref[first + 1] > order_ref[first], 1, 0)
    stretches = (order_ref[first + late], order_ref[first + 1 - late])
    offsets = (
        pl.multiple_of(late * half, half),
        pl.multiple_of((1 - late) * half, half),
    )
    return stretches, offsets


def counts_of(stretches, parity):
    seen = [lax.shift_right_logical(s - parity + 2, 1) for s in stretches]
    return tuple(jnp.maximum(lax.shift_right_logical(n + 1, 1), 1) for n in seen)


def block_of(ref, index, which):
    runs, _, slices, _, grain, _ = ref.shape
    parts = [
        ref[:, 2 * index + u, :, which].astype(F32).reshape(runs * slices * grain, HD)
        for u in range(2)
    ]
    return jnp.concatenate(parts, axis=0).astype(BF16)


def wide(ref, first, count):
    return jnp.concatenate([ref[first + k] for k in range(count)], axis=1)


def forward(keys_ref, parity, stretches, qt_ref, s_ref, e_ref, acc_ref):
    rows, cols = s_ref.shape[1:]
    blocks = keys_ref.shape[1] // 2
    half = rows // 2
    heads = cols // half
    counts = counts_of(stretches, parity)
    bases = (0, blocks)
    shifts = []
    for t in range(2):

        def score(index, peak, masked):
            keys = block_of(keys_ref, index, 0)
            peaks = []
            for c in range(0, heads, GROUP):
                span = slice(c * half, (c + GROUP) * half)
                s = dot(keys, wide(qt_ref, t * heads + c, GROUP), 1, 0)
                if masked:
                    j = lax.broadcasted_iota(jnp.int32, s.shape, 0)
                    r = lax.rem(lax.broadcasted_iota(jnp.int32, s.shape, 1), half)
                    j = j + jnp.where(j >= half, half, 0)
                    ahead = (4 * index + parity - stretches[t]) * half
                    s = jnp.where(j + ahead <= r, s, FILL)
                s_ref[bases[t] + index, :, span] = s
                high = jnp.max(s.reshape(-1, 8, GROUP * half), axis=0)
                peaks.append(jnp.maximum(peak[:, span], high))
            return jnp.concatenate(peaks, axis=1)

        last = counts[t] - 1
        peak = jnp.full((8, cols), FILL, F32)
        peak = lax.fori_loop(0, last, lambda i, p: score(i, p, False), peak)
        peak = score(last, peak, True)
        shifts.append(jnp.max(peak, axis=0, keepdims=True) * RATE)

    results = []
    for t in range(2):

        def weigh(index, total):
            slot = bases[t] + index
            totals = []
            for h in range(heads):
                span = slice(h * half, (h + 1) * half)
                shift = shifts[t][:, span]
                part = total[:, span]
                for start in range(0, rows, CHUNK):
                    chunk = slice(start, start + CHUNK)
                    e = jnp.exp2(s_ref[slot, chunk, span] * RATE - shift)
                    e_ref[slot, h, chunk] = e.astype(BF16)
                    part = part + jnp.sum(e.reshape(-1, 8, half), axis=0)
                totals.append(part)
            return jnp.concatenate(totals, axis=1)

        def attend(index):
            values = block_of(keys_ref, index, 1)
            for c in range(0, heads, GROUP):
                span = slice(c * half, (c + GROUP) * half)
                weights = wide(e_ref.at[bases[t] + index], c, GROUP)
                acc_ref[t, :, span] += dot(values, weights, 0, 0)

        def step(index, total):
            attend(index - 1)
            return weigh(index, total)

        acc_ref[t] = jnp.zeros(acc_ref.shape[1:], F32)
        total = weigh(0, jnp.zeros((8, cols), F32))
        total = lax.fori_loop(1, counts[t], step, total)
        attend(counts[t] - 1)
        results.append((shifts[t], jnp.sum(total, axis=0, keepdims=True)))
    return results


def backward(keys_ref, parity, stretches, qt_ref, gt_ref, delta_ref, e_ref, acc_ref, out_ref):
    runs, pairs, slices, _, grain, _ = keys_ref.shape
    heads = qt_ref.shape[0] // 2
    half = runs * slices * grain
    blocks = pairs // 2
    counts = counts_of(stretches, parity)

    def store(index, which, value):
        for u in range(2):
            part = value[u * half : (u + 1) * half].reshape(runs, slices, grain, HD)
            out_ref[:, 2 * index + u, :, which] = part.astype(BF16)

    def pull(index, both):
        keys = block_of(keys_ref, index, 0)
        values = block_of(keys_ref, index, 1)
        key_term = value_term = 0.0
        for t in range(2 if both else 1):
            slot = index if t == 0 else blocks + index
            for c in range(0, heads, GROUP):
                span = slice(c * half, (c + GROUP) * half)
                weights = wide(e_ref.at[slot], c, GROUP)
                grads = wide(gt_ref, t * heads + c, GROUP)
                slope = dot(values, grads, 1, 0) - delta_ref[t, :, span]
                ds = (weights.astype(F32) * slope).astype(BF16)
                value_term = value_term + dot(grads, weights, 1, 1)
                key_term = key_term + dot(wide(qt_ref, t * heads + c, GROUP), ds, 1, 1)
                acc_ref[t, :, span] += dot(keys, ds, 0, 0)
        store(index, 0, (key_term * SCALE).T)
        store(index, 1, value_term.T)

    @pl.loop(0, counts[1])
    def _(index):
        pull(index, True)

    @pl.loop(counts[1], counts[0])
    def _(index):
        pull(index, False)

    @pl.loop(counts[0], blocks)
    def _(index):
        for which in range(2):
            store(index, which, jnp.zeros((2 * half, HD), F32))


def first_kernel(order_ref, q_ref, keys_ref, qt_ref, e_ref, acc_ref, stat_ref, s_ref):
    half = q_ref.shape[0] // 2
    heads = q_ref.shape[1] // HD
    stretches, offsets = stretches_of(order_ref, half)
    for t in range(2):
        for h in range(heads):
            block = q_ref[pl.ds(offsets[t], half), h * HD : (h + 1) * HD]
            qt_ref[t * heads + h] = flip(block).astype(BF16)
    parity = lax.axis_index("core")
    results = forward(keys_ref, parity, stretches, qt_ref, s_ref, e_ref, acc_ref)
    for t in range(2):
        for k in range(2):
            stat_ref[2 * t + k] = results[t][k]


def second_kernel(
    order_ref,
    g_ref,
    keys_ref,
    qt_ref,
    old_acc_ref,
    old_stat_ref,
    out_ref,
    gt_ref,
    delta_ref,
    dkeys_ref,
    dq_acc_ref,
    s_ref,
    e_ref,
    acc_ref,
    own_gt_ref,
    own_delta_ref,
):
    half = g_ref.shape[0] // 2
    heads = g_ref.shape[1] // HD
    stretches, offsets = stretches_of(order_ref, half)
    parity = 1 - lax.axis_index("core")
    results = forward(keys_ref, parity, stretches, qt_ref, s_ref, e_ref, acc_ref)
    for t in range(2):
        old_shift, old_total = old_stat_ref[2 * t], old_stat_ref[2 * t + 1]
        new_shift, new_total = results[t]
        shift = jnp.maximum(old_shift, new_shift)
        old_part = jnp.exp2(old_shift - shift)
        new_part = jnp.exp2(new_shift - shift)
        inverse = 1.0 / (old_total * old_part + new_total * new_part)
        old_part = old_part * inverse
        new_part = new_part * inverse
        for h in range(heads):
            part = slice(h * half, (h + 1) * half)
            column = slice(h * HD, (h + 1) * HD)
            total = old_acc_ref[t, :, part] * old_part[:, part]
            total = total + acc_ref[t, :, part] * new_part[:, part]
            out = total.astype(BF16)
            out_ref[pl.ds(offsets[t], half), column] = flip(out).astype(BF16)
            grad = flip(g_ref[pl.ds(offsets[t], half), column])
            gt_ref[t * heads + h] = (grad * old_part[:, part]).astype(BF16)
            own_gt_ref[t * heads + h] = (grad * new_part[:, part]).astype(BF16)
            delta = jnp.sum(grad * out.astype(F32), axis=0, keepdims=True)
            delta_ref[t, :, part] = delta * old_part[:, part]
            own_delta_ref[t, :, part] = delta * new_part[:, part]
        dq_acc_ref[t] = jnp.zeros(dq_acc_ref.shape[1:], F32)
    backward(
        keys_ref,
        parity,
        stretches,
        qt_ref,
        own_gt_ref,
        own_delta_ref,
        e_ref,
        dq_acc_ref,
        dkeys_ref,
    )


def third_kernel(
    order_ref,
    keys_ref,
    qt_ref,
    gt_ref,
    delta_ref,
    e_ref,
    old_acc_ref,
    dkeys_ref,
    dq_ref,
    acc_ref,
):
    half = dq_ref.shape[0] // 2
    heads = dq_ref.shape[1] // HD
    stretches, offsets = stretches_of(order_ref, half)
    parity = lax.axis_index("core")
    acc_ref[...] = old_acc_ref[...]
    backward(
        keys_ref,
        parity,
        stretches,
        qt_ref,
        gt_ref,
        delta_ref,
        e_ref,
        acc_ref,
        dkeys_ref,
    )
    for t in range(2):
        for h in range(heads):
            value = (acc_ref[t, :, h * half : (h + 1) * half] * SCALE).T.astype(BF16)
            dq_ref[pl.ds(offsets[t], half), h * HD : (h + 1) * HD] = value


def call(kernel, name, outs, scratch, flops, *args):
    vmem = pl.BlockSpec(memory_space=pltpu.VMEM)
    return pl.pallas_call(
        kernel,
        out_shape=tuple(jax.ShapeDtypeStruct(*out) for out in outs),
        in_specs=[pl.BlockSpec(memory_space=pltpu.SMEM)] + [vmem] * (len(args) - 1),
        out_specs=(vmem,) * len(outs),
        scratch_shapes=[pltpu.VMEM(*item) for item in scratch],
        compiler_params=pltpu.CompilerParams(vmem_limit_bytes=VMEM_BYTES),
        cost_estimate=pl.CostEstimate(
            flops=flops, bytes_accessed=8 << 20, transcendentals=0
        ),
        name=name,
    )(*args)


def shapes_of(queries, keys):
    rows, width = queries.shape
    half = rows // 2
    cols = width // HD * half
    slots = keys.shape[1] // 2 + keys.shape[1] // 4
    heads = cols // half
    return dict(
        weights=((slots, heads, 2 * half, half), BF16),
        scores=((slots, 2 * half, cols), F32),
        flat=((2 * heads, HD, half), BF16),
        acc=((2, HD, cols), F32),
        row=((2, 1, cols), F32),
        stat=((4, 1, cols), F32),
        keys=(keys.shape, BF16),
        queries=(queries.shape, BF16),
    )


def attend_mine(order, queries, mine):
    s = shapes_of(queries, mine)
    outs = (s["flat"], s["weights"], s["acc"], s["stat"])
    return call(
        first_kernel, "first", outs, (s["scores"],), 3 << 30, order, queries, mine
    )


def attend_theirs(order, grads, theirs, qt, acc, stat):
    s = shapes_of(grads, theirs)
    outs = (s["queries"], s["flat"], s["row"], s["keys"], s["acc"])
    scratch = (s["scores"], s["weights"], s["acc"], s["flat"], s["row"])
    return call(
        second_kernel, "second", outs, scratch, 6 << 30, order, grads, theirs, qt, acc, stat
    )


def finish_mine(order, queries, mine, qt, gt, delta, weights, acc):
    s = shapes_of(queries, mine)
    outs = (s["keys"], s["queries"])
    return call(
        third_kernel,
        "third",
        outs,
        (s["acc"],),
        4 << 30,
        order,
        mine,
        qt,
        gt,
        delta,
        weights,
        acc,
    )


AXES = ("zl", "xh", "xl", "core", "y", "zh")
SPREAD = ("y", "zl", "xh", "xl", "zh")
SWAP = ((0, 1), (1, 0))


def per_device(queries, key_vectors, value_vectors, out_grads, pair_order):
    sizes = {name: lax.axis_size(name) for name in AXES}
    runs, zl, xh, xl, zh = (sizes[name] for name in SPREAD)
    rows = key_vectors.shape[0]
    kv_heads = key_vectors.shape[1] // HD
    pairs = zl * xh * xl
    block = (2, rows, HD)

    both = jnp.stack([key_vectors, value_vectors]).reshape(2, rows, kv_heads, HD)
    sent = both.transpose(2, 0, 1, 3).reshape((1, zl, xh, 1, 1) + block)
    sent = jnp.broadcast_to(sent, (runs, zl, xh, xl, zh) + block)
    sent = sent.reshape(runs * pairs * zh, 2 * rows, HD)
    mine = lax.all_to_all(sent, SPREAD, split_axis=0, concat_axis=0, tiled=True)
    mine = mine.reshape((runs, pairs, zh) + block)
    theirs = lax.ppermute(mine, "core", SWAP)

    qt, weights, acc, stat = attend_mine(pair_order, queries, mine)
    attended, gt, delta, dtheirs, acc = attend_theirs(
        pair_order, out_grads, theirs, qt, acc, stat
    )
    other = lax.ppermute(dtheirs, "core", SWAP)
    dmine, query_grads = finish_mine(
        pair_order, queries, mine, qt, gt, delta, weights, acc
    )
    total = (dmine.astype(F32) + other.astype(F32)).astype(BF16)
    total = total.reshape(runs * pairs * zh, 2 * rows, HD)
    got = lax.all_to_all(total, SPREAD, split_axis=0, concat_axis=0, tiled=True)
    got = got.reshape((runs, kv_heads, xl * zh) + block)
    total = got.astype(F32).sum(axis=(0, 2))
    total = total.transpose(1, 2, 0, 3).reshape(2, rows, kv_heads * HD)
    return attended, query_grads, total[0], total[1]


def solution(mesh):
    fine = Mesh(mesh.devices.reshape(4, 2, 2, 2, 8, 2), AXES)
    fsdp, cp = AXES[:4], AXES[4:]
    return jax.shard_map(
        per_device,
        mesh=fine,
        in_specs=(P(cp, fsdp), P(AXES, None), P(AXES, None), P(cp, fsdp), P()),
        out_specs=(P(cp, fsdp), P(cp, fsdp), P(AXES, None), P(AXES, None)),
        check_vma=False,
    )
```

```python
import math
import jax
import jax.numpy as jnp
from jax import lax
from jax.experimental import pallas as pl
from jax.experimental.pallas import tpu as pltpu
from jax.sharding import Mesh, PartitionSpec as P

HD = 128
BF16 = jnp.bfloat16
F32 = jnp.float32
SCALE = 1.0 / math.sqrt(HD)
RATE = SCALE * math.log2(math.e)
FILL = -1e30
VMEM_BYTES = 32 << 20
CHUNK = 64


def dot(a, b, a_axis, b_axis):
    return lax.dot_general(
        a, b, (((a_axis,), (b_axis,)), ((), ())), preferred_element_type=F32
    )


def flip(x):
    return x.astype(F32).T


def stretches_of(order_ref, half):
    first = 2 * (lax.axis_index("y") * lax.axis_size("zh") + lax.axis_index("zh"))
    late = jnp.where(order_ref[first + 1] > order_ref[first], 1, 0)
    stretches = (order_ref[first + late], order_ref[first + 1 - late])
    offsets = (
        pl.multiple_of(late * half, half),
        pl.multiple_of((1 - late) * half, half),
    )
    return stretches, offsets


def counts_of(stretches, parity):
    seen = [lax.shift_right_logical(s - parity + 2, 1) for s in stretches]
    return tuple(jnp.maximum(lax.shift_right_logical(n + 1, 1), 1) for n in seen)


def block_of(ref, index, which):
    runs, _, slices, _, grain, _ = ref.shape
    parts = [
        ref[:, 2 * index + u, :, which].astype(F32).reshape(runs * slices * grain, HD)
        for u in range(2)
    ]
    return jnp.concatenate(parts, axis=0).astype(BF16)


def wide(ref, first, count):
    return jnp.concatenate([ref[first + k] for k in range(count)], axis=1)


def forward(keys_ref, parity, stretches, qt_ref, s_ref, e_ref, acc_ref):
    rows, cols = s_ref.shape[1:]
    blocks = keys_ref.shape[1] // 2
    half = rows // 2
    heads = cols // half
    counts = counts_of(stretches, parity)
    bases = (0, blocks)
    long, short = counts

    def score(t, index, peak, masked):
        keys = block_of(keys_ref, index, 0)
        s = dot(keys, wide(qt_ref, t * heads, heads), 1, 0)
        if masked:
            j = lax.broadcasted_iota(jnp.int32, s.shape, 0)
            r = lax.rem(lax.broadcasted_iota(jnp.int32, s.shape, 1), half)
            j = j + jnp.where(j >= half, half, 0)
            ahead = (4 * index + parity - stretches[t]) * half
            s = jnp.where(j + ahead <= r, s, FILL)
        s_ref[bases[t] + index] = s
        return jnp.maximum(peak, jnp.max(s.reshape(-1, 8, cols), axis=0))

    def weigh(t, index, total):
        slot = bases[t] + index
        totals = []
        for h in range(heads):
            span = slice(h * half, (h + 1) * half)
            part = total[:, span]
            for start in range(0, rows, CHUNK):
                chunk = slice(start, start + CHUNK)
                e = jnp.exp2(s_ref[slot, chunk, span] * RATE - shifts[t][:, span])
                e_ref[slot, h, chunk] = e.astype(BF16)
                part = part + jnp.sum(e.reshape(-1, 8, half), axis=0)
            totals.append(part)
        return jnp.concatenate(totals, axis=1)

    def attend(t, index):
        values = block_of(keys_ref, index, 1)
        weights = wide(e_ref.at[bases[t] + index], 0, heads)
        acc_ref[t] += dot(values, weights, 0, 0)

    def score_both(i, peaks):
        return score(0, i, peaks[0], False), score(1, i, peaks[1], False)

    peak = jnp.full((8, cols), FILL, F32)
    peaks = lax.fori_loop(0, short - 1, score_both, (peak, peak))
    first = lax.fori_loop(
        short - 1, long - 1, lambda i, p: score(0, i, p, False), peaks[0]
    )
    peaks = (score(0, long - 1, first, True), score(1, short - 1, peaks[1], True))
    shifts = [jnp.max(p, axis=0, keepdims=True) * RATE for p in peaks]

    def step_both(i, totals):
        for t in range(2):
            attend(t, i - 1)
        return weigh(0, i, totals[0]), weigh(1, i, totals[1])

    def step_long(i, total):
        attend(0, i - 1)
        return weigh(0, i, total)

    acc_ref[...] = jnp.zeros(acc_ref.shape, F32)
    zero = jnp.zeros((8, cols), F32)
    totals = (weigh(0, 0, zero), weigh(1, 0, zero))
    totals = lax.fori_loop(1, short, step_both, totals)
    last = lax.fori_loop(short, long, step_long, totals[0])
    attend(1, short - 1)
    attend(0, long - 1)
    sums = [jnp.sum(x, axis=0, keepdims=True) for x in (last, totals[1])]
    return list(zip(shifts, sums))


def backward(
    keys_ref, parity, stretches, qt_ref, gt_ref, delta_ref, e_ref, acc_ref, ds_ref, out_ref
):
    runs, pairs, slices, _, grain, _ = keys_ref.shape
    heads = qt_ref.shape[0] // 2
    half = runs * slices * grain
    blocks = pairs // 2
    long, short = counts_of(stretches, parity)

    def store(index, which, value):
        for u in range(2):
            part = value[u * half : (u + 1) * half].reshape(runs, slices, grain, HD)
            out_ref[:, 2 * index + u, :, which] = part.astype(BF16)

    def weights_of(t, index):
        return wide(e_ref.at[index if t == 0 else blocks + index], 0, heads)

    def slopes(index, both):
        values = block_of(keys_ref, index, 1)
        for t in range(2 if both else 1):
            slope = dot(values, wide(gt_ref, t * heads, heads), 1, 0)
            for h in range(heads):
                span = slice(h * half, (h + 1) * half)
                weight = e_ref[index if t == 0 else blocks + index, h].astype(F32)
                part = weight * (slope[:, span] - delta_ref[t, :, span])
                ds_ref[t * heads + h] = part.astype(BF16)

    def finish(index, both):
        keys = block_of(keys_ref, index, 0)
        key_term = value_term = 0.0
        for t in range(2 if both else 1):
            ds = wide(ds_ref, t * heads, heads)
            grads = wide(gt_ref, t * heads, heads)
            value_term = value_term + dot(grads, weights_of(t, index), 1, 1)
            key_term = key_term + dot(wide(qt_ref, t * heads, heads), ds, 1, 1)
            acc_ref[t] += dot(keys, ds, 0, 0)
        store(index, 0, (key_term * SCALE).T)
        store(index, 1, value_term.T)

    slopes(0, True)

    @pl.loop(1, short)
    def _(index):
        finish(index - 1, True)
        slopes(index, True)

    finish(short - 1, True)

    @pl.when(long > short)
    def _():
        slopes(short, False)

        @pl.loop(short + 1, long)
        def _(index):
            finish(index - 1, False)
            slopes(index, False)

        finish(long - 1, False)

    @pl.loop(long, blocks)
    def _(index):
        for which in range(2):
            store(index, which, jnp.zeros((2 * half, HD), F32))


def first_kernel(order_ref, q_ref, keys_ref, qt_ref, e_ref, acc_ref, stat_ref, s_ref):
    half = q_ref.shape[0] // 2
    heads = q_ref.shape[1] // HD
    stretches, offsets = stretches_of(order_ref, half)
    for t in range(2):
        for h in range(heads):
            block = q_ref[pl.ds(offsets[t], half), h * HD : (h + 1) * HD]
            qt_ref[t * heads + h] = flip(block).astype(BF16)
    parity = lax.axis_index("core")
    results = forward(keys_ref, parity, stretches, qt_ref, s_ref, e_ref, acc_ref)
    for t in range(2):
        for k in range(2):
            stat_ref[2 * t + k] = results[t][k]


def second_kernel(
    order_ref,
    g_ref,
    keys_ref,
    qt_ref,
    old_acc_ref,
    old_stat_ref,
    out_ref,
    gt_ref,
    delta_ref,
    dkeys_ref,
    dq_acc_ref,
    s_ref,
    e_ref,
    acc_ref,
    own_gt_ref,
    own_delta_ref,
    ds_ref,
):
    half = g_ref.shape[0] // 2
    heads = g_ref.shape[1] // HD
    stretches, offsets = stretches_of(order_ref, half)
    parity = 1 - lax.axis_index("core")
    results = forward(keys_ref, parity, stretches, qt_ref, s_ref, e_ref, acc_ref)
    for t in range(2):
        old_shift, old_total = old_stat_ref[2 * t], old_stat_ref[2 * t + 1]
        new_shift, new_total = results[t]
        shift = jnp.maximum(old_shift, new_shift)
        old_part = jnp.exp2(old_shift - shift)
        new_part = jnp.exp2(new_shift - shift)
        inverse = 1.0 / (old_total * old_part + new_total * new_part)
        old_part = old_part * inverse
        new_part = new_part * inverse
        for h in range(heads):
            part = slice(h * half, (h + 1) * half)
            column = slice(h * HD, (h + 1) * HD)
            total = old_acc_ref[t, :, part] * old_part[:, part]
            total = total + acc_ref[t, :, part] * new_part[:, part]
            out = total.astype(BF16)
            out_ref[pl.ds(offsets[t], half), column] = flip(out).astype(BF16)
            grad = flip(g_ref[pl.ds(offsets[t], half), column])
            gt_ref[t * heads + h] = (grad * old_part[:, part]).astype(BF16)
            own_gt_ref[t * heads + h] = (grad * new_part[:, part]).astype(BF16)
            delta = jnp.sum(grad * out.astype(F32), axis=0, keepdims=True)
            delta_ref[t, :, part] = delta * old_part[:, part]
            own_delta_ref[t, :, part] = delta * new_part[:, part]
        dq_acc_ref[t] = jnp.zeros(dq_acc_ref.shape[1:], F32)
    backward(
        keys_ref,
        parity,
        stretches,
        qt_ref,
        own_gt_ref,
        own_delta_ref,
        e_ref,
        dq_acc_ref,
        ds_ref,
        dkeys_ref,
    )


def third_kernel(
    order_ref,
    keys_ref,
    qt_ref,
    gt_ref,
    delta_ref,
    e_ref,
    old_acc_ref,
    dkeys_ref,
    dq_ref,
    acc_ref,
    ds_ref,
):
    half = dq_ref.shape[0] // 2
    heads = dq_ref.shape[1] // HD
    stretches, offsets = stretches_of(order_ref, half)
    parity = lax.axis_index("core")
    acc_ref[...] = old_acc_ref[...]
    backward(
        keys_ref,
        parity,
        stretches,
        qt_ref,
        gt_ref,
        delta_ref,
        e_ref,
        acc_ref,
        ds_ref,
        dkeys_ref,
    )
    for t in range(2):
        for h in range(heads):
            value = (acc_ref[t, :, h * half : (h + 1) * half] * SCALE).T.astype(BF16)
            dq_ref[pl.ds(offsets[t], half), h * HD : (h + 1) * HD] = value


def call(kernel, name, outs, scratch, flops, *args):
    vmem = pl.BlockSpec(memory_space=pltpu.VMEM)
    return pl.pallas_call(
        kernel,
        out_shape=tuple(jax.ShapeDtypeStruct(*out) for out in outs),
        in_specs=[pl.BlockSpec(memory_space=pltpu.SMEM)] + [vmem] * (len(args) - 1),
        out_specs=(vmem,) * len(outs),
        scratch_shapes=[pltpu.VMEM(*item) for item in scratch],
        compiler_params=pltpu.CompilerParams(vmem_limit_bytes=VMEM_BYTES),
        cost_estimate=pl.CostEstimate(
            flops=flops, bytes_accessed=8 << 20, transcendentals=0
        ),
        name=name,
    )(*args)


def shapes_of(queries, keys):
    rows, width = queries.shape
    half = rows // 2
    cols = width // HD * half
    slots = keys.shape[1] // 2 + keys.shape[1] // 4
    heads = cols // half
    return dict(
        weights=((slots, heads, 2 * half, half), BF16),
        scores=((slots, 2 * half, cols), F32),
        flat=((2 * heads, HD, half), BF16),
        acc=((2, HD, cols), F32),
        ds=((2 * heads, 2 * half, half), BF16),
        row=((2, 1, cols), F32),
        stat=((4, 1, cols), F32),
        keys=(keys.shape, BF16),
        queries=(queries.shape, BF16),
    )


def attend_mine(order, queries, mine):
    s = shapes_of(queries, mine)
    outs = (s["flat"], s["weights"], s["acc"], s["stat"])
    return call(
        first_kernel, "first", outs, (s["scores"],), 3 << 30, order, queries, mine
    )


def attend_theirs(order, grads, theirs, qt, acc, stat):
    s = shapes_of(grads, theirs)
    outs = (s["queries"], s["flat"], s["row"], s["keys"], s["acc"])
    scratch = (s["scores"], s["weights"], s["acc"], s["flat"], s["row"], s["ds"])
    return call(
        second_kernel, "second", outs, scratch, 6 << 30, order, grads, theirs, qt, acc, stat
    )


def finish_mine(order, queries, mine, qt, gt, delta, weights, acc):
    s = shapes_of(queries, mine)
    outs = (s["keys"], s["queries"])
    return call(
        third_kernel,
        "third",
        outs,
        (s["acc"], s["ds"]),
        4 << 30,
        order,
        mine,
        qt,
        gt,
        delta,
        weights,
        acc,
    )


AXES = ("zl", "xh", "xl", "core", "y", "zh")
SPREAD = ("y", "zl", "xh", "xl", "zh")
SWAP = ((0, 1), (1, 0))


def per_device(queries, key_vectors, value_vectors, out_grads, pair_order):
    sizes = {name: lax.axis_size(name) for name in AXES}
    runs, zl, xh, xl, zh = (sizes[name] for name in SPREAD)
    rows = key_vectors.shape[0]
    kv_heads = key_vectors.shape[1] // HD
    pairs = zl * xh * xl
    block = (2, rows, HD)

    both = jnp.stack([key_vectors, value_vectors]).reshape(2, rows, kv_heads, HD)
    sent = both.transpose(2, 0, 1, 3).reshape((1, zl, xh, 1, 1) + block)
    sent = jnp.broadcast_to(sent, (runs, zl, xh, xl, zh) + block)
    sent = sent.reshape((runs * pairs * zh,) + block)
    mine = lax.all_to_all(sent, SPREAD, split_axis=0, concat_axis=0, tiled=True)
    mine = mine.reshape((runs, pairs, zh) + block)
    theirs = lax.ppermute(mine, "core", SWAP)

    qt, weights, acc, stat = attend_mine(pair_order, queries, mine)
    attended, gt, delta, dtheirs, acc = attend_theirs(
        pair_order, out_grads, theirs, qt, acc, stat
    )
    other = lax.ppermute(dtheirs, "core", SWAP)
    dmine, query_grads = finish_mine(
        pair_order, queries, mine, qt, gt, delta, weights, acc
    )
    total = (dmine.astype(F32) + other.astype(F32)).astype(BF16)
    total = total.reshape((runs * pairs * zh,) + block)
    got = lax.all_to_all(total, SPREAD, split_axis=0, concat_axis=0, tiled=True)
    got = got.reshape((runs, kv_heads, xl * zh) + block)
    total = got.astype(F32).sum(axis=(0, 2))
    total = total.transpose(1, 2, 0, 3).reshape(2, rows, kv_heads * HD)
    return attended, query_grads, total[0], total[1]


def solution(mesh):
    fine = Mesh(mesh.devices.reshape(4, 2, 2, 2, 8, 2), AXES)
    fsdp, cp = AXES[:4], AXES[4:]
    return jax.shard_map(
        per_device,
        mesh=fine,
        in_specs=(P(cp, fsdp), P(AXES, None), P(AXES, None), P(cp, fsdp), P()),
        out_specs=(P(cp, fsdp), P(cp, fsdp), P(AXES, None), P(AXES, None)),
        check_vma=False,
    )
```
